512 devices in a mesh: seq: 4 (over z_lo), fsdp: 32 (over z_hi, y, core), dp: 4 (over x).
Axes of the slice: x: 4, y: 4, z: 16 (z_hi: 4, z_lo: 4; z = z_hi * 4 + z_lo), core: 2. Of those that a mesh axis runs over, the one named last changes fastest.
Arguments:
- query: bfloat16 [128, 768, 1024], P(('fsdp', 'dp'), 'seq'), may hold values from -6 to 6
- key: bfloat16 [128, 768, 1024], P(('fsdp', 'dp'), 'seq'), may hold values from -6 to 6
- value: bfloat16 [128, 768, 1024], P(('fsdp', 'dp'), 'seq'), may hold values from -4 to 4
- out_weight: bfloat16 [1024, 2048], P('fsdp'), may hold values from -0.1875 to 0.1875
- out_grad: bfloat16 [128, 768, 2048], P(('fsdp', 'dp'), 'seq'), may hold values from -5 to 5
- block_ids: int32 [8], P('seq'), may hold values from 0 to 7, as said below
Outputs:
- query_grad: bfloat16 [128, 768, 1024], P(('fsdp', 'dp'), 'seq')
- key_grad: bfloat16 [128, 768, 1024], P(('fsdp', 'dp'), 'seq')
- value_grad: bfloat16 [128, 768, 1024], P(('fsdp', 'dp'), 'seq')
- weight_grad: bfloat16 [1024, 2048], P('fsdp')
The draws below stay inside these ranges and needn't reach their ends.
Inputs may be any that keep to these rules, and one draw needn't show every extreme that they name: `block_ids`: each number 0 to 7 appears once, and entries 2 i and 2 i + 1 always sum to 7.
All inputs are finite; a program needn't handle non-finite values.
Results may differ from the reference program's by a relative error of at most 0.027.
Values may be sent and summed in bfloat16 or wider, within the bound.
No kernel may reach another device: no remote copies, remote signals or barrier semaphores. Data moves between devices by JAX's collectives and lax.ppermute only.
A program may use at most 64 MiB of HBM per device.

```python
import math
import jax
import jax.numpy as jnp
from jax import lax

D = 2048
HEADS = 8
HD = 128
BLOCK = 96
HQ = 1024
TOK_DEV = 192
BLOCKS = 8
LENGTH = 768
SEQS = 128


def float_rows(key, salt):
    noise_key = jax.random.fold_in(key, salt)
    base = jnp.clip(jax.random.normal(noise_key, (SEQS, LENGTH, HQ), jnp.float32), -4.0, 4.0)
    return base


def draw_query(key, part):
    base = float_rows(key, 11)
    return base.astype(jnp.bfloat16)


def draw_key(key, part):
    base = float_rows(key, 12)
    return base.astype(jnp.bfloat16)


def draw_block_ids(key, part):
    pairs = BLOCKS // 2
    order = jax.random.permutation(jax.random.fold_in(key, 7), pairs).astype(jnp.int32)
    flips = jax.random.randint(jax.random.fold_in(key, 8), (pairs,), 0, 2).astype(jnp.int32)
    first = jnp.where(flips == 1, BLOCKS - 1 - order, order)
    return jnp.stack([first, BLOCKS - 1 - first], axis=1).reshape(BLOCKS).astype(jnp.int32)


def block_scale(key, dims, shards, smallest, top_value):
    def one(dim, blocks):
        draws = jax.random.uniform(jax.random.fold_in(jax.random.fold_in(key, 6), dim), (blocks,), jnp.float32, smallest / len(shards), top_value / len(shards))
        return jnp.repeat(jnp.exp(draws), dims[dim] // blocks).reshape((-1,) + (1,) * (len(dims) - dim - 1))

    gain = one(*shards[0])
    for cut in shards[1:]:
        gain = gain * one(*cut)
    return gain


def bell_draw(stream_key, dims, width, reach, cuts=(), kind=jnp.bfloat16):
    drawn = jax.random.normal(stream_key, dims, jnp.float32) * width
    if len(cuts) > 0:
        drawn = block_scale(stream_key, dims, cuts, -0.22, 0.18) * drawn
    return jnp.clip(drawn, min=-reach, max=reach).astype(kind)


def setup_inputs(seed: int = 0) -> dict:
    arg_keys = jax.random.split(jax.random.key(seed), 7)
    query = draw_query(jax.random.fold_in(arg_keys[6], 71), 0)
    key = draw_key(jax.random.fold_in(arg_keys[6], 71), 0)
    value = bell_draw(arg_keys[2], (SEQS, LENGTH, HQ), 1.0, 4.0, ((0, 128), (1, 4)))
    out_weight = bell_draw(arg_keys[3], (HQ, D), HQ ** -0.5, 0.1875, ((0, 32),))
    out_grad = bell_draw(arg_keys[4], (SEQS, LENGTH, D), 1.0, 5.0, ((0, 128), (1, 4)))
    block_ids = draw_block_ids(jax.random.fold_in(arg_keys[6], 71), 0)
    return dict(query=query, key=key, value=value, out_weight=out_weight, out_grad=out_grad, block_ids=block_ids)


def lowered(values):
    return lax.optimization_barrier(values.astype(jnp.bfloat16)).astype(jnp.float32)

def sequence_terms(query_rows, key_rows, value_rows, grad_rows, out_weight, positions):
    score_scale = 1.0 / math.sqrt(HD)
    query_heads = query_rows.astype(jnp.float32).reshape(LENGTH, HEADS, HD)
    key_heads = key_rows.astype(jnp.float32).reshape(LENGTH, HEADS, HD)
    value_heads = value_rows.astype(jnp.float32).reshape(LENGTH, HEADS, HD)
    scores = jnp.einsum('qhd,khd->hqk', query_heads, key_heads) * score_scale
    allowed = positions[None, :] <= positions[:, None]
    scores = jnp.where(allowed[None], scores, -jnp.inf)
    row_top = lax.optimization_barrier(jnp.max(scores, axis=2, keepdims=True))
    row_total = lax.optimization_barrier(jnp.sum(jnp.exp(scores - row_top), axis=2, keepdims=True))
    log_total = row_top + jnp.log(row_total)
    probs = jnp.exp(scores - log_total)
    probs_low = lowered(probs)
    attended = lowered(jnp.einsum('hqk,khd->qhd', probs_low, value_heads))
    attn_grad = lowered(jnp.dot(grad_rows, out_weight.T, preferred_element_type=jnp.float32))
    grad_heads = attn_grad.reshape(LENGTH, HEADS, HD)
    attended_flat = attended.reshape(LENGTH, HQ)
    partials = jnp.einsum('btc,btd->bcd', attended_flat.reshape(-1, TOK_DEV, HQ), grad_rows.astype(jnp.float32).reshape(-1, TOK_DEV, D))
    weight_part = lax.optimization_barrier(jnp.sum(lowered(partials), axis=0))
    row_delta = jnp.einsum('qhd,qhd->hq', grad_heads, attended)
    prob_grad = jnp.einsum('qhd,khd->hqk', grad_heads, value_heads)
    score_grad = lowered(probs * (prob_grad - row_delta[:, :, None]))
    query_grad = (jnp.einsum('hqk,khd->qhd', score_grad, key_heads) * score_scale).astype(jnp.bfloat16)
    key_grad = (jnp.einsum('hqk,qhd->khd', score_grad, query_heads) * score_scale).astype(jnp.bfloat16)
    value_grad = jnp.einsum('hqk,qhd->khd', probs_low, grad_heads).astype(jnp.bfloat16)
    return (query_grad.reshape(LENGTH, HQ), key_grad.reshape(LENGTH, HQ), value_grad.reshape(LENGTH, HQ), weight_part)

def reference(query, key, value, out_weight, out_grad, block_ids):
    offsets = jnp.arange(BLOCK, dtype=jnp.int32)
    positions = (block_ids[:, None].astype(jnp.int32) * BLOCK + offsets[None, :]).reshape(LENGTH)

    def one_sequence(running, inputs):
        results = sequence_terms(inputs[0], inputs[1], inputs[2], inputs[3], out_weight, positions)
        return (running + results[3], (results[0], results[1], results[2]))
    start_sum = jnp.zeros((HQ, D), jnp.float32)
    grad_total, outputs = lax.scan(one_sequence, start_sum, (query, key, value, out_grad))
    weight_grad = (grad_total * (1.0 / math.sqrt(SEQS * LENGTH))).astype(jnp.bfloat16)
    return (outputs[0], outputs[1], outputs[2], weight_grad)
```

```python
import itertools
import math

import jax
import jax.numpy as jnp
from jax import lax
from jax.experimental import pallas as pl
from jax.experimental.pallas import tpu as pltpu
from jax.sharding import Mesh
from jax.sharding import PartitionSpec as P

HD = 128
BF16 = jnp.bfloat16
F32 = jnp.float32
SCALE = 1.0 / math.sqrt(HD)
VMEM = pl.BlockSpec(memory_space=pltpu.VMEM)
SMEM = pl.BlockSpec(memory_space=pltpu.SMEM)
NT = (((1,), (1,)), ((), ()))
NN = (((1,), (0,)), ((), ()))
TN = (((0,), (0,)), ((), ()))


def dot(a, b, dims):
    return lax.dot_general(a, b, dims, preferred_element_type=F32)


def call(kernel, outs, n_scalar, n_vector, name, flops, nbytes, scratch=(), exps=0):
    return pl.pallas_call(
        kernel,
        out_shape=outs,
        in_specs=[SMEM] * n_scalar + [VMEM] * n_vector,
        out_specs=jax.tree.map(lambda _: VMEM, outs),
        scratch_shapes=list(scratch),
        compiler_params=pltpu.CompilerParams(vmem_limit_bytes=40 * 1024 * 1024),
        cost_estimate=pl.CostEstimate(flops=flops, bytes_accessed=nbytes, transcendentals=exps),
        name=name,
    )


def arr(shape, dtype=BF16):
    return jax.ShapeDtypeStruct(shape, dtype)


def group_of(b):
    return 2 * (b % 2) + b // 2


def pack_kernel(where, q_ref, k_ref, v_ref, *outs):
    for k, out in enumerate(outs):
        at = pl.ds(pl.multiple_of(where[k] * 256, 256), 256)
        out[:, 0:256] = q_ref[:, at]
        out[:, 256:512] = k_ref[:, at]
        out[:, 512:768] = v_ref[:, at]


def unpack_kernel(where, r0, r1, r2, r3, dq, dk, dv):
    for k, ref in enumerate((r0, r1, r2, r3)):
        at = pl.ds(pl.multiple_of(where[k] * 256, 256), 256)
        dq[:, at] = ref[:, 0:256]
        dk[:, at] = ref[:, 256:512]
        dv[:, at] = ref[:, 512:768]


def columns_kernel(where, r0, r1, r2, r3, out):
    for k, ref in enumerate((r0, r1, r2, r3)):
        out[:, pl.ds(pl.multiple_of(where[k] * 512, 512), 512)] = ref[...]


def project_kernel(where, own_ref, mate_ref, w_here, w_there, keep, send, w_all):
    first, core = where[0], where[1]
    for k in range(4):
        for c, ref in ((0, w_here), (1, w_there)):
            at = lax.rem(core + c, 2)
            row = pl.multiple_of((where[2 + k] * 2 + at) * 32, 32)
            w_all[first, pl.ds(row, 32), :] = ref[k, 0:32, :]
            w_all[1 - first, pl.ds(row, 32), :] = ref[k, 32:64, :]
    for slot, out in ((1, send), (0, keep)):
        w = w_all[slot]
        out[0:192] = dot(own_ref[...], w, NT).astype(BF16)
        out[192:384] = dot(mate_ref[...], w, NT).astype(BF16)


def positions(ids, shape, dim, first, count):
    at = lax.broadcasted_iota(jnp.int32, shape, dim)
    pos = jnp.zeros(shape, jnp.int32)
    for j in range(count):
        here = (at >= 96 * j) & (at < 96 * (j + 1))
        pos = jnp.where(here, at + (ids[first + j] - j) * 96, pos)
    return pos


def forward_kernel(ids, x0, x1, x2, x3, o_ref, lse_ref, k_all, v_all):
    xs = (x0, x1, x2, x3)
    for i, x in enumerate(xs):
        k_all[192 * i : 192 * i + 192] = x[:, 256:512]
        v_all[192 * i : 192 * i + 192] = x[:, 512:768]
    key_pos = positions(ids, (1, 768), 1, 0, 8)
    for i, x in enumerate(xs):
        rows = slice(192 * i, 192 * i + 192)
        query_pos = positions(ids, (192, 1), 0, 2 * i, 2)
        allowed = key_pos <= query_pos
        for h in range(2):
            cols = slice(HD * h, HD * h + HD)
            s = dot(x[:, cols], k_all[:, cols], NT) * SCALE
            s = jnp.where(allowed, s, -jnp.inf)
            top = jnp.max(s, axis=1, keepdims=True)
            e = jnp.exp(s - top)
            total = jnp.sum(e, axis=1, keepdims=True)
            p = (e * (1.0 / total)).astype(BF16)
            o_ref[rows, cols] = dot(p, v_all[:, cols], NN).astype(BF16)
            lse_ref[rows, cols] = jnp.broadcast_to(top + jnp.log(total), (192, HD))


def backward_kernel(ids, x0, x1, x2, x3, g_near, g_far, o_ref, lse_ref, d0, d1, d2, d3, k_all, v_all, dk, dv):
    xs = (x0, x1, x2, x3)
    ds_ = (d0, d1, d2, d3)
    for i, x in enumerate(xs):
        k_all[192 * i : 192 * i + 192] = x[:, 256:512]
        v_all[192 * i : 192 * i + 192] = x[:, 512:768]
    key_pos = positions(ids, (1, 768), 1, 0, 8)
    for i, x in enumerate(xs):
        rows = slice(192 * i, 192 * i + 192)
        query_pos = positions(ids, (192, 1), 0, 2 * i, 2)
        allowed = key_pos <= query_pos
        grads = g_near if i < 2 else g_far
        grows = slice(192 * (i % 2), 192 * (i % 2) + 192)
        for h in range(2):
            cols = slice(HD * h, HD * h + HD)
            q = x[:, cols]
            g = grads[grows, cols]
            s = dot(q, k_all[:, cols], NT) * SCALE
            p = jnp.exp(jnp.where(allowed, s, -jnp.inf) - lse_ref[rows, HD * h : HD * h + 1])
            delta = jnp.sum(g.astype(F32) * o_ref[rows, cols].astype(F32), axis=1, keepdims=True)
            dp = dot(g, v_all[:, cols], NT)
            ds = (p * (dp - delta)).astype(BF16)
            ds_[i][:, cols] = (dot(ds, k_all[:, cols], NN) * SCALE).astype(BF16)
            pk = dot(ds, q, TN)
            pv = dot(p.astype(BF16), g, TN)
            if i == 0:
                dk[:, cols] = pk
                dv[:, cols] = pv
            else:
                dk[:, cols] += pk
                dv[:, cols] += pv
    for i, d in enumerate(ds_):
        rows = slice(192 * i, 192 * i + 192)
        d[:, 256:512] = (dk[rows] * SCALE).astype(BF16)
        d[:, 512:768] = dv[rows].astype(BF16)


def weight_kernel(where, o_here, o_there, own_ref, mate_ref, keep, send):
    core = where[0]
    for slot, o in ((0, o_here), (1, o_there)):
        for x in range(4):
            cols = slice(512 * x, 512 * x + 512)
            t = (
                dot(o[0:192], own_ref[:, cols], TN) + dot(o[192:384], mate_ref[:, cols], TN)
            ).astype(BF16)
            for y in range(4):
                t0 = t[64 * y : 64 * y + 32]
                t1 = t[64 * y + 32 : 64 * y + 64]
                keep[y, x, slot] = jnp.where(core == 0, t0, t1)
                send[y, x, slot] = jnp.where(core == 0, t1, t0)


def nearest(dests, source_of, n=16):
    pairs = []
    for row in range(4):
        takers = [d for d in dests if source_of(*d) == row]
        best = None
        for columns in itertools.permutations(range(4), len(takers)):
            steps = 0
            for (a, b), c in zip(takers, columns):
                gap = abs((4 * a + b) - (4 * row + c))
                steps += min(gap, n - gap) ** 2
            if best is None or steps < best[0]:
                best = (steps, columns)
        for (a, b), c in zip(takers, best[1]):
            pairs.append((c * 4 + row, b * 4 + a))
    return pairs


def swap(value, axis, mask, n):
    return lax.ppermute(value, axis, [(i, i ^ mask) for i in range(n)])


def shards(query, key, value, out_weight, out_grad, block_ids):
    b, a = lax.axis_index("seq"), lax.axis_index("zh")
    y, core, x = lax.axis_index("y"), lax.axis_index("c"), lax.axis_index("dp")
    half, pair = b % 2, b // 2
    places = [(i, j) for i in range(4) for j in range(4)]
    z = ("seq", "zh")

    first = lax.ppermute(
        out_weight, z, nearest([d for d in places if d[0] // 2 != d[1] % 2], lambda i, j: i ^ 2)
    )
    second = lax.ppermute(
        out_weight, z, nearest(places, lambda i, j: i ^ 1 if i // 2 == j % 2 else i ^ 3)
    )
    grads = out_grad[0]
    groups = jnp.stack([group_of(b ^ k) for k in range(4)]).astype(jnp.int32)
    packed = call(pack_kernel, [arr((192, 768))] * 4, 1, 3, "pack", 0, 2400000)(
        groups, query[0], key[0], value[0]
    )
    rows = [packed[0]] + [swap(packed[k], "seq", k, 4) for k in (1, 2, 3)]
    mate_grads = swap(grads, "seq", 1, 4)
    first = jnp.where(a // 2 == half, out_weight, first)
    piece = jnp.concatenate([first, second], axis=0)
    w_here = jnp.stack([piece] + [swap(piece, "y", k, 4) for k in (1, 2, 3)])
    w_there = swap(w_here, "c", 1, 2)
    all_ids = lax.all_gather(block_ids, "seq", axis=0, tiled=False)
    ids = jnp.concatenate([all_ids[b ^ k] for k in range(4)])

    slots = jnp.stack([(a % 2) ^ pair, core] + [y ^ k for k in range(4)]).astype(jnp.int32)
    g_near, g_send = call(
        project_kernel,
        [arr((384, 256))] * 2,
        1,
        4,
        "project",
        2 * 384 * 2048 * 512,
        4500000,
        [pltpu.VMEM((2, 256, 2048), BF16)],
    )(slots, grads, mate_grads, w_here, w_there)
    g_far = swap(g_send, "seq", 2, 4)
    kv = [pltpu.VMEM((768, 256), BF16)] * 2
    attended, lse = call(
        forward_kernel,
        [arr((768, 256)), arr((768, 256), F32)],
        1,
        4,
        "forward",
        4 * 2 * 768 * 768 * 128,
        2400000,
        kv,
        2 * 768 * 768,
    )(ids, *rows)
    o_there = swap(attended[384:768], "seq", 2, 4)
    back = call(
        backward_kernel,
        [arr((192, 768))] * 4,
        1,
        8,
        "backward",
        10 * 2 * 768 * 768 * 128,
        4000000,
        kv + [pltpu.VMEM((768, 256), F32)] * 2,
        2 * 768 * 768,
    )(ids, *rows, g_near, g_far, attended, lse)
    home = [back[0]] + [swap(back[k], "seq", k, 4) for k in (1, 2, 3)]
    query_grad, key_grad, value_grad = call(
        unpack_kernel, [arr((192, 1024))] * 3, 1, 4, "unpack", 0, 2400000
    )(groups, *home)

    keep, send = call(
        weight_kernel, [arr((4, 4, 2, 32, 512))] * 2, 1, 4, "weight", 2 * 384 * 2048 * 512, 4500000
    )(core.astype(jnp.int32)[None], attended[0:384], o_there, grads, mate_grads)
    taken = swap(send, "c", 1, 2)
    both = (keep.astype(F32) + taken.astype(F32)).astype(BF16).reshape(16, 2, 32, 512)
    parts = lax.all_to_all(both, ("y", "dp"), 0, 0, tiled=True)
    mine = jnp.sum(parts.astype(F32), axis=0).astype(BF16)
    turn = [(i * 4 + j, group_of(j) * 4 + group_of(i)) for i in range(4) for j in range(4)]
    turn2 = [(i * 4 + j, group_of(j) * 4 + (group_of(i) ^ 1)) for i in range(4) for j in range(4)]
    line = (lax.ppermute(mine[0], z, turn).astype(F32) + lax.ppermute(mine[1], z, turn2).astype(F32)).astype(BF16)
    near = [swap(line, "seq", k, 4).astype(F32) for k in (1, 2, 3)]
    total = (line.astype(F32) + near[0]) + (near[1] + near[2])
    quarter = (total * (1.0 / math.sqrt(192 * 512))).astype(BF16)
    quarters = [quarter] + [swap(quarter, "dp", k, 4) for k in (1, 2, 3)]
    columns = jnp.stack([x ^ k for k in range(4)]).astype(jnp.int32)
    weight_grad = call(columns_kernel, arr((32, 2048)), 1, 4, "columns", 0, 300000)(
        columns, *quarters
    )
    return query_grad[None], key_grad[None], value_grad[None], weight_grad


def solution(mesh):
    fine = Mesh(mesh.devices.reshape(4, 4, 4, 2, 4), ("seq", "zh", "y", "c", "dp"))
    tokens = P(("zh", "y", "c", "dp"), "seq", None)
    rows = P(("zh", "y", "c"), None)
    return jax.shard_map(
        shards,
        mesh=fine,
        in_specs=(tokens, tokens, tokens, rows, tokens, P("seq")),
        out_specs=(tokens, tokens, tokens, rows),
        check_vma=False,
    )
```

```python
import itertools
import math

import jax
import jax.numpy as jnp
from jax import lax
from jax.experimental import pallas as pl
from jax.experimental.pallas import tpu as pltpu
from jax.sharding import Mesh
from jax.sharding import PartitionSpec as P

HD = 128
BF16 = jnp.bfloat16
F32 = jnp.float32
SCALE = 1.0 / math.sqrt(HD)
VMEM = pl.BlockSpec(memory_space=pltpu.VMEM)
SMEM = pl.BlockSpec(memory_space=pltpu.SMEM)
NT = (((1,), (1,)), ((), ()))
NN = (((1,), (0,)), ((), ()))
TN = (((0,), (0,)), ((), ()))


def dot(a, b, dims):
    return lax.dot_general(a, b, dims, preferred_element_type=F32)


def call(kernel, outs, n_scalar, n_vector, name, scratch=()):
    return pl.pallas_call(
        kernel,
        out_shape=outs,
        in_specs=[SMEM] * n_scalar + [VMEM] * n_vector,
        out_specs=jax.tree.map(lambda _: VMEM, outs),
        scratch_shapes=list(scratch),
        compiler_params=pltpu.CompilerParams(vmem_limit_bytes=40 * 1024 * 1024),
        cost_estimate=pl.CostEstimate(flops=1000, bytes_accessed=1000, transcendentals=0),
        name=name,
    )


def arr(shape, dtype=BF16):
    return jax.ShapeDtypeStruct(shape, dtype)


def group_of(b):
    return 2 * (b % 2) + b // 2


def pack_kernel(ids, q_ref, k_ref, v_ref, out):
    lane = lax.broadcasted_iota(jnp.int32, (8, 768), 1)
    block = jnp.where(lane < 384, ids[0], ids[1]).astype(F32).astype(BF16)
    for j in range(4):
        cols = slice(256 * group_of(j), 256 * group_of(j) + 256)
        out[j, 0:192, 0:256] = q_ref[:, cols]
        out[j, 0:192, 256:512] = k_ref[:, cols]
        out[j, 0:192, 512:768] = v_ref[:, cols]
        out[j, 192:200, :] = block


def unpack_kernel(home, dq, dk, dv):
    for j in range(4):
        cols = slice(256 * group_of(j), 256 * group_of(j) + 256)
        dq[:, cols] = home[j, :, 0:256]
        dk[:, cols] = home[j, :, 256:512]
        dv[:, cols] = home[j, :, 512:768]


def quarter_kernel(parts, out):
    t = [parts[j].astype(F32) for j in range(4)]
    total = ((t[0] + t[1]) + (t[2] + t[3])) * (1.0 / math.sqrt(192 * 512))
    for x in range(4):
        out[x] = total.astype(BF16)


def finish_kernel(parts, out):
    for x in range(4):
        out[:, 512 * x : 512 * x + 512] = parts[x]


def project_kernel(where, own_ref, mate_ref, w_here, w_there, keep, send, w_all):
    first, core = where[0], where[1]
    for k in range(4):
        for c, ref in ((0, w_here), (1, w_there)):
            row = pl.multiple_of((2 * where[2 + k] + lax.rem(core + c, 2)) * 32, 32)
            w_all[first, pl.ds(row, 32), :] = ref[k, 0:32, :]
            w_all[1 - first, pl.ds(row, 32), :] = ref[k, 32:64, :]
    for slot, out in ((1, send), (0, keep)):
        w = w_all[slot]
        out[0:192] = dot(own_ref[...], w, NT).astype(BF16)
        out[192:384] = dot(mate_ref[...], w, NT).astype(BF16)


def positions(x, shape, dim):
    at = lax.broadcasted_iota(jnp.int32, shape, dim)
    first = x[192:200, 0:128].astype(F32).astype(jnp.int32)[0:1, 0:1]
    second = x[192:200, 384:512].astype(F32).astype(jnp.int32)[0:1, 0:1]
    return jnp.where(at < 96, first * 96 + at, second * 96 + (at - 96))


def forward_kernel(where, x_all, near, far, lse_ref, k_all, v_all):
    xs = [x_all.at[where[0] ^ i] for i in range(4)]
    for i, x in enumerate(xs):
        k_all[192 * i : 192 * i + 192] = x[0:192, 256:512]
        v_all[192 * i : 192 * i + 192] = x[0:192, 512:768]
    key_pos = jnp.concatenate([positions(x, (1, 192), 1) for x in xs], axis=1)
    for i, x in enumerate(xs):
        rows = slice(192 * i, 192 * i + 192)
        here = slice(192 * (i % 2), 192 * (i % 2) + 192)
        allowed = key_pos <= positions(x, (192, 1), 0)
        for h in range(2):
            cols = slice(HD * h, HD * h + HD)
            s = dot(x[0:192, cols], k_all[:, cols], NT) * SCALE
            s = jnp.where(allowed, s, -jnp.inf)
            top = jnp.max(s, axis=1, keepdims=True)
            e = jnp.exp(s - top)
            total = jnp.sum(e, axis=1, keepdims=True)
            p = (e * (1.0 / total)).astype(BF16)
            out = near if i < 2 else far
            out[here, cols] = dot(p, v_all[:, cols], NN).astype(BF16)
            lse_ref[rows, cols] = jnp.broadcast_to(top + jnp.log(total), (192, HD))


def backward_kernel(
    where, x_all, g_near, g_far, o_near, o_far, lse_ref, home, k_all, v_all, dk, dv
):
    xs = [x_all.at[where[0] ^ i] for i in range(4)]
    outs = [home.at[where[0] ^ i] for i in range(4)]
    for i, x in enumerate(xs):
        k_all[192 * i : 192 * i + 192] = x[0:192, 256:512]
        v_all[192 * i : 192 * i + 192] = x[0:192, 512:768]
    key_pos = jnp.concatenate([positions(x, (1, 192), 1) for x in xs], axis=1)
    for i, x in enumerate(xs):
        rows = slice(192 * i, 192 * i + 192)
        here = slice(192 * (i % 2), 192 * (i % 2) + 192)
        grads, attended = (g_near, o_near) if i < 2 else (g_far, o_far)
        allowed = key_pos <= positions(x, (192, 1), 0)
        for h in range(2):
            cols = slice(HD * h, HD * h + HD)
            q = x[0:192, cols]
            g = grads[here, cols]
            s = dot(q, k_all[:, cols], NT) * SCALE
            p = jnp.exp(jnp.where(allowed, s, -jnp.inf) - lse_ref[rows, HD * h : HD * h + 1])
            delta = jnp.sum(g.astype(F32) * attended[here, cols].astype(F32), axis=1, keepdims=True)
            dp = dot(g, v_all[:, cols], NT)
            ds = (p * (dp - delta)).astype(BF16)
            outs[i][:, cols] = (dot(ds, k_all[:, cols], NN) * SCALE).astype(BF16)
            pk = dot(ds, q, TN)
            pv = dot(p.astype(BF16), g, TN)
            if i == 0:
                dk[:, cols] = pk
                dv[:, cols] = pv
            else:
                dk[:, cols] += pk
                dv[:, cols] += pv
    for i, out in enumerate(outs):
        rows = slice(192 * i, 192 * i + 192)
        out[:, 256:512] = (dk[rows] * SCALE).astype(BF16)
        out[:, 512:768] = dv[rows].astype(BF16)


def weight_kernel(where, o_here, o_there, own_ref, mate_ref, keep, send):
    core = where[0]
    for slot, o in ((0, o_here), (1, o_there)):
        for x in range(4):
            cols = slice(512 * x, 512 * x + 512)
            t = dot(o[0:192], own_ref[:, cols], TN) + dot(o[192:384], mate_ref[:, cols], TN)
            t = t.astype(BF16)
            for y in range(4):
                t0 = t[64 * y : 64 * y + 32]
                t1 = t[64 * y + 32 : 64 * y + 64]
                keep[y, x, slot] = jnp.where(core == 0, t0, t1)
                send[y, x, slot] = jnp.where(core == 0, t1, t0)


def sum_kernel(parts, own, other):
    for slot, out in ((0, own), (1, other)):
        t = [parts[j, slot].astype(F32) for j in range(16)]
        while len(t) > 1:
            t = [t[i] + t[i + 1] for i in range(0, len(t), 2)]
        out[...] = t[0].astype(BF16)


def nearest(dests, source_of, n=16):
    pairs = []
    for row in range(4):
        takers = [d for d in dests if source_of(*d) == row]
        best = None
        for columns in itertools.permutations(range(4), len(takers)):
            steps = 0
            for (a, b), c in zip(takers, columns):
                gap = abs((4 * a + b) - (4 * row + c))
                steps += min(gap, n - gap) ** 2
            if best is None or steps < best[0]:
                best = (steps, columns)
        for (a, b), c in zip(takers, best[1]):
            pairs.append((c * 4 + row, b * 4 + a))
    return pairs


def swap(value, axis, mask, n):
    return lax.ppermute(value, axis, [(i, i ^ mask) for i in range(n)])


def scalars(*values):
    return jnp.stack(values).astype(jnp.int32)


def exchange(value, axes):
    return lax.all_to_all(value, axes, 0, 0, tiled=True)


def shards(query, key, value, out_weight, out_grad, block_ids):
    b, a = lax.axis_index("seq"), lax.axis_index("zh")
    y, core = lax.axis_index("y"), lax.axis_index("c")
    half, pair = b & 1, b >> 1
    places = [(i, j) for i in range(4) for j in range(4)]
    z = ("seq", "zh")

    grads = out_grad[0]
    mate_grads = swap(grads, "seq", 1, 4)

    first = lax.ppermute(
        out_weight, z, nearest([d for d in places if d[0] // 2 != d[1] % 2], lambda i, j: i ^ 2)
    )
    second = lax.ppermute(
        out_weight, z, nearest(places, lambda i, j: i ^ 1 if i // 2 == j % 2 else i ^ 3)
    )
    packed = call(pack_kernel, arr((4, 200, 768)), 1, 3, "pack")(
        block_ids, query[0], key[0], value[0]
    )
    packed, mate_grads, first, second = lax.optimization_barrier(
        (packed, mate_grads, first, second)
    )
    rows = exchange(packed, "seq")
    first = jnp.where((a >> 1) == half, out_weight, first)
    piece = jnp.concatenate([first, second], axis=0)
    pieces = [piece] + [swap(piece, "y", k, 4) for k in (1, 2, 3)]
    w_here = jnp.stack(pieces)
    rows, w_here = lax.optimization_barrier((rows, w_here))
    w_there = swap(w_here, "c", 1, 2)

    g_near, g_send = call(
        project_kernel, [arr((384, 256))] * 2, 1, 4, "project", [pltpu.VMEM((2, 256, 2048), BF16)]
    )(scalars((a & 1) ^ pair, core, *(y ^ k for k in range(4))), grads, mate_grads, w_here, w_there)
    g_far = swap(g_send, "seq", 2, 4)
    kv = [pltpu.VMEM((768, 256), BF16)] * 2
    o_near, o_far, lse = call(
        forward_kernel, [arr((384, 256))] * 2 + [arr((768, 256), F32)], 1, 1, "forward", kv
    )(scalars(b), rows)
    o_there = swap(o_far, "seq", 2, 4)
    o_there, _ = lax.optimization_barrier((o_there, g_send))
    keep, send = call(weight_kernel, [arr((4, 4, 2, 32, 512))] * 2, 1, 4, "weight")(
        scalars(core), o_near, o_there, grads, mate_grads
    )
    send, g_far = lax.optimization_barrier((send, g_far))
    taken = swap(send, "c", 1, 2)
    back = call(
        backward_kernel,
        arr((4, 192, 768)),
        1,
        6,
        "backward",
        kv + [pltpu.VMEM((768, 256), F32)] * 2,
    )(scalars(b), rows, g_near, g_far, o_near, o_far, lse)
    home = exchange(back, "seq")
    both = (keep.astype(F32) + taken.astype(F32)).astype(BF16).reshape(16, 2, 32, 512)
    parts = exchange(both, ("y", "dp"))
    own, other = call(sum_kernel, [arr((32, 512))] * 2, 0, 1, "sum")(parts)
    turn = [(i * 4 + j, group_of(j) * 4 + group_of(i)) for i in range(4) for j in range(4)]
    turn2 = [(i * 4 + j, group_of(j) * 4 + (group_of(i) ^ 1)) for i in range(4) for j in range(4)]
    line = lax.ppermute(own, z, turn).astype(F32) + lax.ppermute(other, z, turn2).astype(F32)
    line, home = lax.optimization_barrier((line, home))
    spread = jnp.broadcast_to(line.astype(BF16)[None], (4, 32, 512))
    quarter = call(quarter_kernel, arr((4, 32, 512)), 0, 1, "quarter")(exchange(spread, "seq"))
    weight_grad = call(finish_kernel, arr((32, 2048)), 0, 1, "finish")(exchange(quarter, "dp"))
    query_grad, key_grad, value_grad = call(unpack_kernel, [arr((192, 1024))] * 3, 0, 1, "unpack")(
        home
    )
    return query_grad[None], key_grad[None], value_grad[None], weight_grad


def solution(mesh):
    fine = Mesh(mesh.devices.reshape(4, 4, 4, 2, 4), ("seq", "zh", "y", "c", "dp"))
    tokens = P(("zh", "y", "c", "dp"), "seq", None)
    rows = P(("zh", "y", "c"), None)
    return jax.shard_map(
        shards,
        mesh=fine,
        in_specs=(tokens, tokens, tokens, rows, tokens, P("seq")),
        out_specs=(tokens, tokens, tokens, rows),
        check_vma=False,
    )
```

```python
import itertools
import math

import jax
import jax.numpy as jnp
from jax import lax
from jax.experimental import pallas as pl
from jax.experimental.pallas import tpu as pltpu
from jax.sharding import Mesh
from jax.sharding import PartitionSpec as P

HD = 128
BF16 = jnp.bfloat16
F32 = jnp.float32
SCALE = 1.0 / math.sqrt(HD)
VMEM = pl.BlockSpec(memory_space=pltpu.VMEM)
SMEM = pl.BlockSpec(memory_space=pltpu.SMEM)
NT = (((1,), (1,)), ((), ()))
NN = (((1,), (0,)), ((), ()))
TN = (((0,), (0,)), ((), ()))


def dot(a, b, dims):
    return lax.dot_general(a, b, dims, preferred_element_type=F32)


def call(kernel, outs, n_scalar, n_vector, name, scratch=()):
    return pl.pallas_call(
        kernel,
        out_shape=outs,
        in_specs=[SMEM] * n_scalar + [VMEM] * n_vector,
        out_specs=jax.tree.map(lambda _: VMEM, outs),
        scratch_shapes=list(scratch),
        compiler_params=pltpu.CompilerParams(vmem_limit_bytes=40 * 1024 * 1024),
        cost_estimate=pl.CostEstimate(flops=1000, bytes_accessed=1000, transcendentals=0),
        name=name,
    )


def arr(shape, dtype=BF16):
    return jax.ShapeDtypeStruct(shape, dtype)


def group_of(b):
    return 2 * (b % 2) + b // 2


def pack_kernel(ids, q_ref, k_ref, v_ref, out):
    lane = lax.broadcasted_iota(jnp.int32, (8, 768), 1)
    block = jnp.where(lane < 384, ids[0], ids[1]).astype(F32).astype(BF16)
    for j in range(4):
        cols = slice(256 * group_of(j), 256 * group_of(j) + 256)
        out[j, 0:192, 0:256] = q_ref[:, cols]
        out[j, 0:192, 256:512] = k_ref[:, cols]
        out[j, 0:192, 512:768] = v_ref[:, cols]
        out[j, 192:200, :] = block


def unpack_kernel(home, dq, dk, dv):
    for j in range(4):
        cols = slice(256 * group_of(j), 256 * group_of(j) + 256)
        dq[:, cols] = home[j, :, 0:256]
        dk[:, cols] = home[j, :, 256:512]
        dv[:, cols] = home[j, :, 512:768]


def quarter_kernel(parts, out):
    t = [parts[j].astype(F32) for j in range(4)]
    total = (t[0] + t[1]) + (t[2] + t[3])
    out[...] = (total * (1.0 / math.sqrt(192 * 512))).astype(BF16)


def finish_kernel(where, p0, p1, p2, p3, out):
    for k, ref in enumerate((p0, p1, p2, p3)):
        out[:, pl.ds(pl.multiple_of(where[k] * 512, 512), 512)] = ref[...]


def project_kernel(where, own_ref, mate_ref, w_here, w_there, keep, send, w_all):
    first, core = where[0], where[1]
    for k in range(4):
        for c, ref in ((0, w_here), (1, w_there)):
            row = pl.multiple_of((2 * where[2 + k] + lax.rem(core + c, 2)) * 32, 32)
            w_all[first, pl.ds(row, 32), :] = ref[k, 0:32, :]
            w_all[1 - first, pl.ds(row, 32), :] = ref[k, 32:64, :]
    for slot, out in ((1, send), (0, keep)):
        w = w_all[slot]
        out[0:192] = dot(own_ref[...], w, NT).astype(BF16)
        out[192:384] = dot(mate_ref[...], w, NT).astype(BF16)


def positions(x, shape, dim):
    at = lax.broadcasted_iota(jnp.int32, shape, dim)
    first = x[192:200, 0:128].astype(F32).astype(jnp.int32)[0:1, 0:1]
    second = x[192:200, 384:512].astype(F32).astype(jnp.int32)[0:1, 0:1]
    return jnp.where(at < 96, first * 96 + at, second * 96 + (at - 96))


def forward_kernel(where, x_all, near, far, lse_ref, k_all, v_all):
    xs = [x_all.at[where[0] ^ i] for i in range(4)]
    for i, x in enumerate(xs):
        k_all[192 * i : 192 * i + 192] = x[0:192, 256:512]
        v_all[192 * i : 192 * i + 192] = x[0:192, 512:768]
    key_pos = jnp.concatenate([positions(x, (1, 192), 1) for x in xs], axis=1)
    for i, x in enumerate(xs):
        rows = slice(192 * i, 192 * i + 192)
        here = slice(192 * (i % 2), 192 * (i % 2) + 192)
        allowed = key_pos <= positions(x, (192, 1), 0)
        for h in range(2):
            cols = slice(HD * h, HD * h + HD)
            s = dot(x[0:192, cols], k_all[:, cols], NT) * SCALE
            s = jnp.where(allowed, s, -jnp.inf)
            top = jnp.max(s, axis=1, keepdims=True)
            e = jnp.exp(s - top)
            total = jnp.sum(e, axis=1, keepdims=True)
            p = (e * (1.0 / total)).astype(BF16)
            out = near if i < 2 else far
            out[here, cols] = dot(p, v_all[:, cols], NN).astype(BF16)
            lse_ref[rows, cols] = jnp.broadcast_to(top + jnp.log(total), (192, HD))


def backward_kernel(
    where, x_all, g_near, g_far, o_near, o_far, lse_ref, home, k_all, v_all, dk, dv
):
    xs = [x_all.at[where[0] ^ i] for i in range(4)]
    outs = [home.at[where[0] ^ i] for i in range(4)]
    for i, x in enumerate(xs):
        k_all[192 * i : 192 * i + 192] = x[0:192, 256:512]
        v_all[192 * i : 192 * i + 192] = x[0:192, 512:768]
    key_pos = jnp.concatenate([positions(x, (1, 192), 1) for x in xs], axis=1)
    for i, x in enumerate(xs):
        rows = slice(192 * i, 192 * i + 192)
        here = slice(192 * (i % 2), 192 * (i % 2) + 192)
        grads, attended = (g_near, o_near) if i < 2 else (g_far, o_far)
        allowed = key_pos <= positions(x, (192, 1), 0)
        for h in range(2):
            cols = slice(HD * h, HD * h + HD)
            q = x[0:192, cols]
            g = grads[here, cols]
            s = dot(q, k_all[:, cols], NT) * SCALE
            p = jnp.exp(jnp.where(allowed, s, -jnp.inf) - lse_ref[rows, HD * h : HD * h + 1])
            delta = jnp.sum(g.astype(F32) * attended[here, cols].astype(F32), axis=1, keepdims=True)
            dp = dot(g, v_all[:, cols], NT)
            ds = (p * (dp - delta)).astype(BF16)
            outs[i][:, cols] = (dot(ds, k_all[:, cols], NN) * SCALE).astype(BF16)
            pk = dot(ds, q, TN)
            pv = dot(p.astype(BF16), g, TN)
            if i == 0:
                dk[:, cols] = pk
                dv[:, cols] = pv
            else:
                dk[:, cols] += pk
                dv[:, cols] += pv
    for i, out in enumerate(outs):
        rows = slice(192 * i, 192 * i + 192)
        out[:, 256:512] = (dk[rows] * SCALE).astype(BF16)
        out[:, 512:768] = dv[rows].astype(BF16)


def weight_kernel(where, o_here, o_there, own_ref, mate_ref, keep, send):
    core = where[0]
    for slot, o in ((0, o_here), (1, o_there)):
        for x in range(4):
            cols = slice(512 * x, 512 * x + 512)
            t = dot(o[0:192], own_ref[:, cols], TN) + dot(o[192:384], mate_ref[:, cols], TN)
            t = t.astype(BF16)
            for y in range(4):
                t0 = t[64 * y : 64 * y + 32]
                t1 = t[64 * y + 32 : 64 * y + 64]
                keep[y, x, slot] = jnp.where(core == 0, t0, t1)
                send[y, x, slot] = jnp.where(core == 0, t1, t0)


def sum_kernel(parts, own, other):
    for slot, out in ((0, own), (1, other)):
        t = [parts[j, slot].astype(F32) for j in range(16)]
        while len(t) > 1:
            t = [t[i] + t[i + 1] for i in range(0, len(t), 2)]
        out[...] = t[0].astype(BF16)


def nearest(dests, source_of, n=16):
    pairs = []
    for row in range(4):
        takers = [d for d in dests if source_of(*d) == row]
        best = None
        for columns in itertools.permutations(range(4), len(takers)):
            steps = 0
            for (a, b), c in zip(takers, columns):
                gap = abs((4 * a + b) - (4 * row + c))
                steps += min(gap, n - gap) ** 2
            if best is None or steps < best[0]:
                best = (steps, columns)
        for (a, b), c in zip(takers, best[1]):
            pairs.append((c * 4 + row, b * 4 + a))
    return pairs


def swap(value, axis, mask, n):
    return lax.ppermute(value, axis, [(i, i ^ mask) for i in range(n)])


def scalars(*values):
    return jnp.stack(values).astype(jnp.int32)


def exchange(value, axes):
    return lax.all_to_all(value, axes, 0, 0, tiled=True)


def shards(query, key, value, out_weight, out_grad, block_ids):
    b, a = lax.axis_index("seq"), lax.axis_index("zh")
    y, core, x = lax.axis_index("y"), lax.axis_index("c"), lax.axis_index("dp")
    half, pair = b & 1, b >> 1
    places = [(i, j) for i in range(4) for j in range(4)]
    z = ("seq", "zh")

    grads = out_grad[0]

    first = lax.ppermute(
        out_weight, z, nearest([d for d in places if d[0] // 2 != d[1] % 2], lambda i, j: i ^ 2)
    )
    second = lax.ppermute(
        out_weight, z, nearest(places, lambda i, j: i ^ 1 if i // 2 == j % 2 else i ^ 3)
    )
    packed = call(pack_kernel, arr((4, 200, 768)), 1, 3, "pack")(
        block_ids, query[0], key[0], value[0]
    )
    rows = exchange(packed, "seq")
    grads, first, second = lax.optimization_barrier((grads, first, second))
    mate_grads = swap(grads, "seq", 1, 4)
    first = jnp.where((a >> 1) == half, out_weight, first)
    piece = jnp.concatenate([first, second], axis=0)
    pieces = [piece] + [swap(piece, "y", k, 4) for k in (1, 2, 3)]
    w_here = jnp.stack(pieces)
    w_there = swap(w_here, "c", 1, 2)

    g_near, g_send = call(
        project_kernel, [arr((384, 256))] * 2, 1, 4, "project", [pltpu.VMEM((2, 256, 2048), BF16)]
    )(scalars((a & 1) ^ pair, core, *(y ^ k for k in range(4))), grads, mate_grads, w_here, w_there)
    g_far = swap(g_send, "seq", 2, 4)
    kv = [pltpu.VMEM((768, 256), BF16)] * 2
    o_near, o_far, lse = call(
        forward_kernel, [arr((384, 256))] * 2 + [arr((768, 256), F32)], 1, 1, "forward", kv
    )(scalars(b), rows)
    o_there = swap(o_far, "seq", 2, 4)
    o_there, _ = lax.optimization_barrier((o_there, pieces))
    keep, send = call(weight_kernel, [arr((4, 4, 2, 32, 512))] * 2, 1, 4, "weight")(
        scalars(core), o_near, o_there, grads, mate_grads
    )
    taken = swap(send, "c", 1, 2)
    back = call(
        backward_kernel,
        arr((4, 192, 768)),
        1,
        6,
        "backward",
        kv + [pltpu.VMEM((768, 256), F32)] * 2,
    )(scalars(b), rows, g_near, g_far, o_near, o_far, lse)
    both = (keep.astype(F32) + taken.astype(F32)).astype(BF16).reshape(16, 2, 32, 512)
    parts = exchange(both, ("y", "dp"))
    own, other = call(sum_kernel, [arr((32, 512))] * 2, 0, 1, "sum")(parts)
    own, other, g_far = lax.optimization_barrier((own, other, g_far))
    turn = [(i * 4 + j, group_of(j) * 4 + group_of(i)) for i in range(4) for j in range(4)]
    turn2 = [(i * 4 + j, group_of(j) * 4 + (group_of(i) ^ 1)) for i in range(4) for j in range(4)]
    line = lax.ppermute(own, z, turn).astype(F32) + lax.ppermute(other, z, turn2).astype(F32)
    spread = jnp.broadcast_to(line.astype(BF16)[None], (4, 32, 512))
    quarter = call(quarter_kernel, arr((32, 512)), 0, 1, "quarter")(exchange(spread, "seq"))
    back, quarter = lax.optimization_barrier((back, quarter))
    home = exchange(back, "seq")
    quarters = [quarter] + [swap(quarter, "dp", k, 4) for k in (1, 2, 3)]
    weight_grad = call(finish_kernel, arr((32, 2048)), 1, 4, "finish")(
        scalars(*(x ^ k for k in range(4))), *quarters
    )
    query_grad, key_grad, value_grad = call(unpack_kernel, [arr((192, 1024))] * 3, 0, 1, "unpack")(
        home
    )
    return query_grad[None], key_grad[None], value_grad[None], weight_grad


def solution(mesh):
    fine = Mesh(mesh.devices.reshape(4, 4, 4, 2, 4), ("seq", "zh", "y", "c", "dp"))
    tokens = P(("zh", "y", "c", "dp"), "seq", None)
    rows = P(("zh", "y", "c"), None)
    return jax.shard_map(
        shards,
        mesh=fine,
        in_specs=(tokens, tokens, tokens, rows, tokens, P("seq")),
        out_specs=(tokens, tokens, tokens, rows),
        check_vma=False,
    )
```

```python
import itertools
import math

import jax
import jax.numpy as jnp
from jax import lax
from jax.experimental import pallas as pl
from jax.experimental.pallas import tpu as pltpu
from jax.sharding import Mesh
from jax.sharding import PartitionSpec as P

HD = 128
BF16 = jnp.bfloat16
F32 = jnp.float32
SCALE = 1.0 / math.sqrt(HD)
VMEM = pl.BlockSpec(memory_space=pltpu.VMEM)
SMEM = pl.BlockSpec(memory_space=pltpu.SMEM)
NT = (((1,), (1,)), ((), ()))
NN = (((1,), (0,)), ((), ()))
TN = (((0,), (0,)), ((), ()))


def dot(a, b, dims):
    return lax.dot_general(a, b, dims, preferred_element_type=F32)


def call(kernel, outs, n_scalar, n_vector, name, scratch=()):
    return pl.pallas_call(
        kernel,
        out_shape=outs,
        in_specs=[SMEM] * n_scalar + [VMEM] * n_vector,
        out_specs=jax.tree.map(lambda _: VMEM, outs),
        scratch_shapes=list(scratch),
        compiler_params=pltpu.CompilerParams(vmem_limit_bytes=40 * 1024 * 1024),
        cost_estimate=pl.CostEstimate(flops=1000, bytes_accessed=1000, transcendentals=0),
        name=name,
    )


def arr(shape, dtype=BF16):
    return jax.ShapeDtypeStruct(shape, dtype)


def group_of(b):
    return 2 * (b % 2) + b // 2


def pack_kernel(ids, q_ref, k_ref, v_ref, out):
    lane = lax.broadcasted_iota(jnp.int32, (8, 768), 1)
    block = jnp.where(lane < 384, ids[0], ids[1]).astype(F32).astype(BF16)
    for j in range(4):
        cols = slice(256 * group_of(j), 256 * group_of(j) + 256)
        out[j, 0:192, 0:256] = q_ref[:, cols]
        out[j, 0:192, 256:512] = k_ref[:, cols]
        out[j, 0:192, 512:768] = v_ref[:, cols]
        out[j, 192:200, :] = block


def unpack_kernel(home, dq, dk, dv):
    for j in range(4):
        cols = slice(256 * group_of(j), 256 * group_of(j) + 256)
        dq[:, cols] = home[j, :, 0:256]
        dk[:, cols] = home[j, :, 256:512]
        dv[:, cols] = home[j, :, 512:768]


def quarter_kernel(p0, p1, p2, p3, out):
    t = [ref[...].astype(F32) for ref in (p0, p1, p2, p3)]
    total = (t[0] + t[1]) + (t[2] + t[3])
    out[...] = (total * (1.0 / math.sqrt(192 * 512))).astype(BF16)


def finish_kernel(where, p0, p1, p2, p3, out):
    for k, ref in enumerate((p0, p1, p2, p3)):
        out[:, pl.ds(pl.multiple_of(where[k] * 512, 512), 512)] = ref[...]


def project_kernel(where, own_ref, mate_ref, w_here, w_there, keep, send, w_all):
    first, core = where[0], where[1]
    for k in range(4):
        for c, ref in ((0, w_here), (1, w_there)):
            row = pl.multiple_of((2 * where[2 + k] + lax.rem(core + c, 2)) * 32, 32)
            w_all[first, pl.ds(row, 32), :] = ref[k, 0:32, :]
            w_all[1 - first, pl.ds(row, 32), :] = ref[k, 32:64, :]
    for slot, out in ((1, send), (0, keep)):
        w = w_all[slot]
        out[0:192] = dot(own_ref[...], w, NT).astype(BF16)
        out[192:384] = dot(mate_ref[...], w, NT).astype(BF16)


def positions(x, shape, dim):
    at = lax.broadcasted_iota(jnp.int32, shape, dim)
    first = x[192:200, 0:128].astype(F32).astype(jnp.int32)[0:1, 0:1]
    second = x[192:200, 384:512].astype(F32).astype(jnp.int32)[0:1, 0:1]
    return jnp.where(at < 96, first * 96 + at, second * 96 + (at - 96))


def forward_kernel(where, x_all, near, far, lse_ref, k_all, v_all):
    xs = [x_all.at[where[0] ^ i] for i in range(4)]
    for i, x in enumerate(xs):
        k_all[192 * i : 192 * i + 192] = x[0:192, 256:512]
        v_all[192 * i : 192 * i + 192] = x[0:192, 512:768]
    key_pos = jnp.concatenate([positions(x, (1, 192), 1) for x in xs], axis=1)
    for i, x in enumerate(xs):
        rows = slice(192 * i, 192 * i + 192)
        here = slice(192 * (i % 2), 192 * (i % 2) + 192)
        allowed = key_pos <= positions(x, (192, 1), 0)
        for h in range(2):
            cols = slice(HD * h, HD * h + HD)
            s = dot(x[0:192, cols], k_all[:, cols], NT) * SCALE
            s = jnp.where(allowed, s, -jnp.inf)
            top = jnp.max(s, axis=1, keepdims=True)
            e = jnp.exp(s - top)
            total = jnp.sum(e, axis=1, keepdims=True)
            p = (e * (1.0 / total)).astype(BF16)
            out = near if i < 2 else far
            out[here, cols] = dot(p, v_all[:, cols], NN).astype(BF16)
            lse_ref[rows, cols] = jnp.broadcast_to(top + jnp.log(total), (192, HD))


def backward_kernel(
    where, x_all, g_near, g_far, o_near, o_far, lse_ref, home, k_all, v_all, dk, dv
):
    xs = [x_all.at[where[0] ^ i] for i in range(4)]
    outs = [home.at[where[0] ^ i] for i in range(4)]
    for i, x in enumerate(xs):
        k_all[192 * i : 192 * i + 192] = x[0:192, 256:512]
        v_all[192 * i : 192 * i + 192] = x[0:192, 512:768]
    key_pos = jnp.concatenate([positions(x, (1, 192), 1) for x in xs], axis=1)
    for i, x in enumerate(xs):
        rows = slice(192 * i, 192 * i + 192)
        here = slice(192 * (i % 2), 192 * (i % 2) + 192)
        grads, attended = (g_near, o_near) if i < 2 else (g_far, o_far)
        allowed = key_pos <= positions(x, (192, 1), 0)
        for h in range(2):
            cols = slice(HD * h, HD * h + HD)
            q = x[0:192, cols]
            g = grads[here, cols]
            s = dot(q, k_all[:, cols], NT) * SCALE
            p = jnp.exp(jnp.where(allowed, s, -jnp.inf) - lse_ref[rows, HD * h : HD * h + 1])
            delta = jnp.sum(g.astype(F32) * attended[here, cols].astype(F32), axis=1, keepdims=True)
            dp = dot(g, v_all[:, cols], NT)
            ds = (p * (dp - delta)).astype(BF16)
            outs[i][:, cols] = (dot(ds, k_all[:, cols], NN) * SCALE).astype(BF16)
            pk = dot(ds, q, TN)
            pv = dot(p.astype(BF16), g, TN)
            if i == 0:
                dk[:, cols] = pk
                dv[:, cols] = pv
            else:
                dk[:, cols] += pk
                dv[:, cols] += pv
    for i, out in enumerate(outs):
        rows = slice(192 * i, 192 * i + 192)
        out[:, 256:512] = (dk[rows] * SCALE).astype(BF16)
        out[:, 512:768] = dv[rows].astype(BF16)


def weight_kernel(where, o_here, o_there, own_ref, mate_ref, keep, send):
    core = where[0]
    for slot, o in ((0, o_here), (1, o_there)):
        for x in range(4):
            cols = slice(512 * x, 512 * x + 512)
            t = dot(o[0:192], own_ref[:, cols], TN) + dot(o[192:384], mate_ref[:, cols], TN)
            t = t.astype(BF16)
            for y in range(4):
                t0 = t[64 * y : 64 * y + 32]
                t1 = t[64 * y + 32 : 64 * y + 64]
                keep[y, x, slot] = jnp.where(core == 0, t0, t1)
                send[y, x, slot] = jnp.where(core == 0, t1, t0)


def sum_kernel(parts, own, other):
    for slot, out in ((0, own), (1, other)):
        t = [parts[j, slot].astype(F32) for j in range(16)]
        while len(t) > 1:
            t = [t[i] + t[i + 1] for i in range(0, len(t), 2)]
        out[...] = t[0].astype(BF16)


def nearest(dests, source_of, n=16):
    pairs = []
    for row in range(4):
        takers = [d for d in dests if source_of(*d) == row]
        best = None
        for columns in itertools.permutations(range(4), len(takers)):
            steps = 0
            for (a, b), c in zip(takers, columns):
                gap = abs((4 * a + b) - (4 * row + c))
                steps += min(gap, n - gap) ** 2
            if best is None or steps < best[0]:
                best = (steps, columns)
        for (a, b), c in zip(takers, best[1]):
            pairs.append((c * 4 + row, b * 4 + a))
    return pairs


def swap(value, axis, mask, n):
    return lax.ppermute(value, axis, [(i, i ^ mask) for i in range(n)])


def scalars(*values):
    return jnp.stack(values).astype(jnp.int32)


def exchange(value, axes):
    return lax.all_to_all(value, axes, 0, 0, tiled=True)


def shards(query, key, value, out_weight, out_grad, block_ids):
    b, a = lax.axis_index("seq"), lax.axis_index("zh")
    y, core, x = lax.axis_index("y"), lax.axis_index("c"), lax.axis_index("dp")
    half, pair = b & 1, b >> 1
    places = [(i, j) for i in range(4) for j in range(4)]
    z = ("seq", "zh")

    grads = out_grad[0]

    first = lax.ppermute(
        out_weight, z, nearest([d for d in places if d[0] // 2 != d[1] % 2], lambda i, j: i ^ 2)
    )
    second = lax.ppermute(
        out_weight, z, nearest(places, lambda i, j: i ^ 1 if i // 2 == j % 2 else i ^ 3)
    )
    packed = call(pack_kernel, arr((4, 200, 768)), 1, 3, "pack")(
        block_ids, query[0], key[0], value[0]
    )
    rows = exchange(packed, "seq")
    grads, first, second = lax.optimization_barrier((grads, first, second))
    mate_grads = swap(grads, "seq", 1, 4)
    first = jnp.where((a >> 1) == half, out_weight, first)
    piece = jnp.concatenate([first, second], axis=0)
    pieces = [piece] + [swap(piece, "y", k, 4) for k in (1, 2, 3)]
    w_here = jnp.stack(pieces)
    w_there = swap(w_here, "c", 1, 2)

    g_near, g_send = call(
        project_kernel, [arr((384, 256))] * 2, 1, 4, "project", [pltpu.VMEM((2, 256, 2048), BF16)]
    )(scalars((a & 1) ^ pair, core, *(y ^ k for k in range(4))), grads, mate_grads, w_here, w_there)
    g_far = swap(g_send, "seq", 2, 4)
    kv = [pltpu.VMEM((768, 256), BF16)] * 2
    o_near, o_far, lse = call(
        forward_kernel, [arr((384, 256))] * 2 + [arr((768, 256), F32)], 1, 1, "forward", kv
    )(scalars(b), rows)
    o_there = swap(o_far, "seq", 2, 4)
    o_there, _ = lax.optimization_barrier((o_there, pieces))
    keep, send = call(weight_kernel, [arr((4, 4, 2, 32, 512))] * 2, 1, 4, "weight")(
        scalars(core), o_near, o_there, grads, mate_grads
    )
    taken = swap(send, "c", 1, 2)
    back = call(
        backward_kernel,
        arr((4, 192, 768)),
        1,
        6,
        "backward",
        kv + [pltpu.VMEM((768, 256), F32)] * 2,
    )(scalars(b), rows, g_near, g_far, o_near, o_far, lse)
    both = (keep.astype(F32) + taken.astype(F32)).astype(BF16).reshape(16, 2, 32, 512)
    parts = exchange(both, ("y", "dp"))
    own, other = call(sum_kernel, [arr((32, 512))] * 2, 0, 1, "sum")(parts)
    turn = [(i * 4 + j, group_of(j) * 4 + group_of(i)) for i in range(4) for j in range(4)]
    turn2 = [(i * 4 + j, group_of(j) * 4 + (group_of(i) ^ 1)) for i in range(4) for j in range(4)]
    line = lax.ppermute(own, z, turn).astype(F32) + lax.ppermute(other, z, turn2).astype(F32)
    line = line.astype(BF16)
    back, line = lax.optimization_barrier((back, line))
    home = exchange(back, "seq")
    lines = [line] + [swap(line, "seq", k, 4) for k in (1, 2, 3)]
    quarter = call(quarter_kernel, arr((32, 512)), 0, 4, "quarter")(*lines)
    quarters = [quarter] + [swap(quarter, "dp", k, 4) for k in (1, 2, 3)]
    weight_grad = call(finish_kernel, arr((32, 2048)), 1, 4, "finish")(
        scalars(*(x ^ k for k in range(4))), *quarters
    )
    query_grad, key_grad, value_grad = call(unpack_kernel, [arr((192, 1024))] * 3, 0, 1, "unpack")(
        home
    )
    return query_grad[None], key_grad[None], value_grad[None], weight_grad


def solution(mesh):
    fine = Mesh(mesh.devices.reshape(4, 4, 4, 2, 4), ("seq", "zh", "y", "c", "dp"))
    tokens = P(("zh", "y", "c", "dp"), "seq", None)
    rows = P(("zh", "y", "c"), None)
    return jax.shard_map(
        shards,
        mesh=fine,
        in_specs=(tokens, tokens, tokens, rows, tokens, P("seq")),
        out_specs=(tokens, tokens, tokens, rows),
        check_vma=False,
    )
```

```python
import itertools
import math

import jax
import jax.numpy as jnp
from jax import lax
from jax.experimental import pallas as pl
from jax.experimental.pallas import tpu as pltpu
from jax.sharding import Mesh
from jax.sharding import PartitionSpec as P

HD = 128
BF16 = jnp.bfloat16
F32 = jnp.float32
SCALE = 1.0 / math.sqrt(HD)
VMEM = pl.BlockSpec(memory_space=pltpu.VMEM)
SMEM = pl.BlockSpec(memory_space=pltpu.SMEM)
NT = (((1,), (1,)), ((), ()))
NN = (((1,), (0,)), ((), ()))
TN = (((0,), (0,)), ((), ()))


def dot(a, b, dims):
    return lax.dot_general(a, b, dims, preferred_element_type=F32)


def call(kernel, outs, n_scalar, n_vector, name, scratch=()):
    return pl.pallas_call(
        kernel,
        out_shape=outs,
        in_specs=[SMEM] * n_scalar + [VMEM] * n_vector,
        out_specs=jax.tree.map(lambda _: VMEM, outs),
        scratch_shapes=list(scratch),
        compiler_params=pltpu.CompilerParams(vmem_limit_bytes=40 * 1024 * 1024),
        cost_estimate=pl.CostEstimate(flops=1000, bytes_accessed=1000, transcendentals=0),
        name=name,
    )


def arr(shape, dtype=BF16):
    return jax.ShapeDtypeStruct(shape, dtype)


def group_of(b):
    return 2 * (b % 2) + b // 2


def pack_kernel(ids, q_ref, k_ref, v_ref, out, block, sems):
    copies = []
    for j in range(4):
        cols = pl.ds(256 * group_of(j), 256)
        for n, ref in enumerate((q_ref, k_ref, v_ref)):
            to = out.at[j, pl.ds(0, 192), pl.ds(256 * n, 256)]
            copies.append(pltpu.make_async_copy(ref.at[:, cols], to, sems.at[4 * j + n]))
            copies[-1].start()
    lane = lax.broadcasted_iota(jnp.int32, (8, 768), 1)
    block[...] = jnp.where(lane < 384, ids[0], ids[1]).astype(F32).astype(BF16)
    for j in range(4):
        to = out.at[j, pl.ds(192, 8), :]
        copies.append(pltpu.make_async_copy(block, to, sems.at[4 * j + 3]))
        copies[-1].start()
    for copy in copies:
        copy.wait()


def unpack_kernel(home, dq, dk, dv):
    for j in range(4):
        cols = slice(256 * group_of(j), 256 * group_of(j) + 256)
        dq[:, cols] = home[j, :, 0:256]
        dk[:, cols] = home[j, :, 256:512]
        dv[:, cols] = home[j, :, 512:768]


def quarter_kernel(parts, out):
    t = [parts[j].astype(F32) for j in range(4)]
    total = ((t[0] + t[1]) + (t[2] + t[3])) * (1.0 / math.sqrt(192 * 512))
    for x in range(4):
        out[x] = total.astype(BF16)


def finish_kernel(parts, out):
    for x in range(4):
        out[:, 512 * x : 512 * x + 512] = parts[x]


def project_kernel(where, own_ref, mate_ref, w0, w1, w2, w3, keep, send, w_all):
    first, core = where[0], where[1]
    for k, ref in enumerate((w0, w1, w2, w3)):
        for c in range(2):
            row = pl.multiple_of((2 * where[2 + k] + lax.rem(core + c, 2)) * 32, 32)
            w_all[first, pl.ds(row, 32), :] = ref[c, 0:32, :]
            w_all[1 - first, pl.ds(row, 32), :] = ref[c, 32:64, :]
    for slot, out in ((1, send), (0, keep)):
        w = w_all[slot]
        out[0:192] = dot(own_ref[...], w, NT).astype(BF16)
        out[192:384] = dot(mate_ref[...], w, NT).astype(BF16)


def positions(x, shape, dim):
    at = lax.broadcasted_iota(jnp.int32, shape, dim)
    first = x[192:200, 0:128].astype(F32).astype(jnp.int32)[0:1, 0:1]
    second = x[192:200, 384:512].astype(F32).astype(jnp.int32)[0:1, 0:1]
    return jnp.where(at < 96, first * 96 + at, second * 96 + (at - 96))


def forward_kernel(where, x_all, near, far, lse_ref, k_all, v_all):
    xs = [x_all.at[where[0] ^ i] for i in range(4)]
    for i, x in enumerate(xs):
        k_all[192 * i : 192 * i + 192] = x[0:192, 256:512]
        v_all[192 * i : 192 * i + 192] = x[0:192, 512:768]
    key_pos = jnp.concatenate([positions(x, (1, 192), 1) for x in xs], axis=1)
    for i, x in enumerate(xs):
        rows = slice(192 * i, 192 * i + 192)
        here = slice(192 * (i % 2), 192 * (i % 2) + 192)
        allowed = key_pos <= positions(x, (192, 1), 0)
        for h in range(2):
            cols = slice(HD * h, HD * h + HD)
            s = dot(x[0:192, cols], k_all[:, cols], NT) * SCALE
            s = jnp.where(allowed, s, -jnp.inf)
            top = jnp.max(s, axis=1, keepdims=True)
            e = jnp.exp(s - top)
            total = jnp.sum(e, axis=1, keepdims=True)
            p = (e * (1.0 / total)).astype(BF16)
            out = near if i < 2 else far
            out[here, cols] = dot(p, v_all[:, cols], NN).astype(BF16)
            lse_ref[rows, cols] = jnp.broadcast_to(top + jnp.log(total), (192, HD))


def backward_kernel(
    where, x_all, g_near, g_far, o_near, o_far, lse_ref, home, k_all, v_all, dk, dv
):
    xs = [x_all.at[where[0] ^ i] for i in range(4)]
    outs = [home.at[where[0] ^ i] for i in range(4)]
    for i, x in enumerate(xs):
        k_all[192 * i : 192 * i + 192] = x[0:192, 256:512]
        v_all[192 * i : 192 * i + 192] = x[0:192, 512:768]
    key_pos = jnp.concatenate([positions(x, (1, 192), 1) for x in xs], axis=1)
    for i, x in enumerate(xs):
        rows = slice(192 * i, 192 * i + 192)
        here = slice(192 * (i % 2), 192 * (i % 2) + 192)
        grads, attended = (g_near, o_near) if i < 2 else (g_far, o_far)
        allowed = key_pos <= positions(x, (192, 1), 0)
        for h in range(2):
            cols = slice(HD * h, HD * h + HD)
            q = x[0:192, cols]
            g = grads[here, cols]
            s = dot(q, k_all[:, cols], NT) * SCALE
            p = jnp.exp(jnp.where(allowed, s, -jnp.inf) - lse_ref[rows, HD * h : HD * h + 1])
            delta = jnp.sum(g.astype(F32) * attended[here, cols].astype(F32), axis=1, keepdims=True)
            dp = dot(g, v_all[:, cols], NT)
            ds = (p * (dp - delta)).astype(BF16)
            outs[i][:, cols] = (dot(ds, k_all[:, cols], NN) * SCALE).astype(BF16)
            pk = dot(ds, q, TN)
            pv = dot(p.astype(BF16), g, TN)
            if i == 0:
                dk[:, cols] = pk
                dv[:, cols] = pv
            else:
                dk[:, cols] += pk
                dv[:, cols] += pv
    for i, out in enumerate(outs):
        rows = slice(192 * i, 192 * i + 192)
        out[:, 256:512] = (dk[rows] * SCALE).astype(BF16)
        out[:, 512:768] = dv[rows].astype(BF16)


def weight_kernel(where, o_here, o_there, own_ref, mate_ref, keep, send):
    core = where[0]
    for slot, o in ((0, o_here), (1, o_there)):
        for x in range(4):
            cols = slice(512 * x, 512 * x + 512)
            t = dot(o[0:192], own_ref[:, cols], TN) + dot(o[192:384], mate_ref[:, cols], TN)
            t = t.astype(BF16)
            for y in range(4):
                t0 = t[64 * y : 64 * y + 32]
                t1 = t[64 * y + 32 : 64 * y + 64]
                keep[y, x, slot] = jnp.where(core == 0, t0, t1)
                send[y, x, slot] = jnp.where(core == 0, t1, t0)


def sum_kernel(parts, own, other):
    for slot, out in ((0, own), (1, other)):
        t = [parts[j, slot].astype(F32) for j in range(16)]
        while len(t) > 1:
            t = [t[i] + t[i + 1] for i in range(0, len(t), 2)]
        out[...] = t[0].astype(BF16)


def nearest(dests, source_of, n=16):
    pairs = []
    for row in range(4):
        takers = [d for d in dests if source_of(*d) == row]
        best = None
        for columns in itertools.permutations(range(4), len(takers)):
            steps = 0
            for (a, b), c in zip(takers, columns):
                gap = abs((4 * a + b) - (4 * row + c))
                steps += min(gap, n - gap) ** 2
            if best is None or steps < best[0]:
                best = (steps, columns)
        for (a, b), c in zip(takers, best[1]):
            pairs.append((c * 4 + row, b * 4 + a))
    return pairs


def swap(value, axis, mask, n):
    return lax.ppermute(value, axis, [(i, i ^ mask) for i in range(n)])


def scalars(*values):
    return jnp.stack(values).astype(jnp.int32)


def exchange(value, axes):
    return lax.all_to_all(value, axes, 0, 0, tiled=True)


def shards(query, key, value, out_weight, out_grad, block_ids):
    b, a = lax.axis_index("seq"), lax.axis_index("zh")
    y, core = lax.axis_index("y"), lax.axis_index("c")
    half, pair = b & 1, b >> 1
    places = [(i, j) for i in range(4) for j in range(4)]
    z = ("seq", "zh")

    grads = out_grad[0]

    first = lax.ppermute(
        out_weight, z, nearest([d for d in places if d[0] // 2 != d[1] % 2], lambda i, j: i ^ 2)
    )
    second = lax.ppermute(
        out_weight, z, nearest(places, lambda i, j: i ^ 1 if i // 2 == j % 2 else i ^ 3)
    )
    anywhere = pl.BlockSpec(memory_space=pl.ANY)
    packed = pl.pallas_call(
        pack_kernel,
        out_shape=arr((4, 200, 768)),
        in_specs=[SMEM] + [anywhere] * 3,
        out_specs=anywhere,
        scratch_shapes=[pltpu.VMEM((8, 768), BF16), pltpu.SemaphoreType.DMA((16,))],
        compiler_params=pltpu.CompilerParams(vmem_limit_bytes=60 * 1024 * 1024),
        cost_estimate=pl.CostEstimate(flops=1000, bytes_accessed=1000, transcendentals=0),
        name="pack",
    )(block_ids, query[0], key[0], value[0])
    rows = exchange(packed, "seq")
    grads, first, second = lax.optimization_barrier((grads, first, second))
    mate_grads = swap(grads, "seq", 1, 4)
    first = jnp.where((a >> 1) == half, out_weight, first)
    piece = jnp.concatenate([first, second], axis=0)
    both_cores = jnp.stack([piece, swap(piece, "c", 1, 2)])
    pieces = [both_cores] + [swap(both_cores, "y", k, 4) for k in (1, 2, 3)]

    g_near, g_send = call(
        project_kernel, [arr((384, 256))] * 2, 1, 6, "project", [pltpu.VMEM((2, 256, 2048), BF16)]
    )(scalars((a & 1) ^ pair, core, *(y ^ k for k in range(4))), grads, mate_grads, *pieces)
    g_far = swap(g_send, "seq", 2, 4)
    kv = [pltpu.VMEM((768, 256), BF16)] * 2
    o_near, o_far, lse = call(
        forward_kernel, [arr((384, 256))] * 2 + [arr((768, 256), F32)], 1, 1, "forward", kv
    )(scalars(b), rows)
    o_there = swap(o_far, "seq", 2, 4)
    o_there, _ = lax.optimization_barrier((o_there, pieces))
    keep, send = call(weight_kernel, [arr((4, 4, 2, 32, 512))] * 2, 1, 4, "weight")(
        scalars(core), o_near, o_there, grads, mate_grads
    )
    taken = swap(send, "c", 1, 2)
    back = call(
        backward_kernel,
        arr((4, 192, 768)),
        1,
        6,
        "backward",
        kv + [pltpu.VMEM((768, 256), F32)] * 2,
    )(scalars(b), rows, g_near, g_far, o_near, o_far, lse)
    home = exchange(back, "seq")
    both = (keep.astype(F32) + taken.astype(F32)).astype(BF16).reshape(16, 2, 32, 512)
    both, g_send = lax.optimization_barrier((both, g_send))
    parts = exchange(both, ("y", "dp"))
    own, other = call(sum_kernel, [arr((32, 512))] * 2, 0, 1, "sum")(parts)
    turn = [(i * 4 + j, group_of(j) * 4 + group_of(i)) for i in range(4) for j in range(4)]
    turn2 = [(i * 4 + j, group_of(j) * 4 + (group_of(i) ^ 1)) for i in range(4) for j in range(4)]
    line = lax.ppermute(own, z, turn).astype(F32) + lax.ppermute(other, z, turn2).astype(F32)
    line, home = lax.optimization_barrier((line, home))
    spread = jnp.broadcast_to(line.astype(BF16)[None], (4, 32, 512))
    quarter = call(quarter_kernel, arr((4, 32, 512)), 0, 1, "quarter")(exchange(spread, "seq"))
    weight_grad = call(finish_kernel, arr((32, 2048)), 0, 1, "finish")(exchange(quarter, "dp"))
    query_grad, key_grad, value_grad = call(unpack_kernel, [arr((192, 1024))] * 3, 0, 1, "unpack")(
        home
    )
    return query_grad[None], key_grad[None], value_grad[None], weight_grad


def solution(mesh):
    fine = Mesh(mesh.devices.reshape(4, 4, 4, 2, 4), ("seq", "zh", "y", "c", "dp"))
    tokens = P(("zh", "y", "c", "dp"), "seq", None)
    rows = P(("zh", "y", "c"), None)
    return jax.shard_map(
        shards,
        mesh=fine,
        in_specs=(tokens, tokens, tokens, rows, tokens, P("seq")),
        out_specs=(tokens, tokens, tokens, rows),
        check_vma=False,
    )
```

```python
import itertools
import math

import jax
import jax.numpy as jnp
from jax import lax
from jax.experimental import pallas as pl
from jax.experimental.pallas import tpu as pltpu
from jax.sharding import Mesh
from jax.sharding import PartitionSpec as P

HD = 128
BF16 = jnp.bfloat16
F32 = jnp.float32
SCALE = 1.0 / math.sqrt(HD)
VMEM = pl.BlockSpec(memory_space=pltpu.VMEM)
SMEM = pl.BlockSpec(memory_space=pltpu.SMEM)
NT = (((1,), (1,)), ((), ()))
NN = (((1,), (0,)), ((), ()))
TN = (((0,), (0,)), ((), ()))


def dot(a, b, dims):
    return lax.dot_general(a, b, dims, preferred_element_type=F32)


def call(kernel, outs, n_scalar, n_vector, name, scratch=()):
    return pl.pallas_call(
        kernel,
        out_shape=outs,
        in_specs=[SMEM] * n_scalar + [VMEM] * n_vector,
        out_specs=jax.tree.map(lambda _: VMEM, outs),
        scratch_shapes=list(scratch),
        compiler_params=pltpu.CompilerParams(vmem_limit_bytes=40 * 1024 * 1024),
        cost_estimate=pl.CostEstimate(flops=1000, bytes_accessed=1000, transcendentals=0),
        name=name,
    )


def arr(shape, dtype=BF16):
    return jax.ShapeDtypeStruct(shape, dtype)


def group_of(b):
    return 2 * (b % 2) + b // 2


def pack_kernel(ids, q_ref, k_ref, v_ref, out, sems):
    copies = []
    for j in range(4):
        cols = pl.ds(256 * group_of(j), 256)
        for n, ref in enumerate((q_ref, k_ref, v_ref)):
            to = out.at[j, pl.ds(0, 192), pl.ds(256 * n, 256)]
            copies.append(pltpu.make_async_copy(ref.at[:, cols], to, sems.at[3 * j + n]))
            copies[-1].start()
    lane = lax.broadcasted_iota(jnp.int32, (8, 768), 1)
    block = jnp.where(lane < 384, ids[0], ids[1]).astype(F32).astype(BF16)
    for j in range(4):
        out[j, 192:200, :] = block
    for copy in copies:
        copy.wait()


def unpack_kernel(home, dq, dk, dv):
    for j in range(4):
        cols = slice(256 * group_of(j), 256 * group_of(j) + 256)
        dq[:, cols] = home[j, :, 0:256]
        dk[:, cols] = home[j, :, 256:512]
        dv[:, cols] = home[j, :, 512:768]


def quarter_kernel(parts, out):
    t = [parts[j].astype(F32) for j in range(4)]
    total = ((t[0] + t[1]) + (t[2] + t[3])) * (1.0 / math.sqrt(192 * 512))
    for x in range(4):
        out[x] = total.astype(BF16)


def finish_kernel(parts, out):
    for x in range(4):
        out[:, 512 * x : 512 * x + 512] = parts[x]


def project_kernel(where, own_ref, mate_ref, w_here, w_there, keep, send, w_all):
    first, core = where[0], where[1]
    for k in range(4):
        for c, ref in ((0, w_here), (1, w_there)):
            row = pl.multiple_of((2 * where[2 + k] + lax.rem(core + c, 2)) * 32, 32)
            w_all[first, pl.ds(row, 32), :] = ref[k, 0:32, :]
            w_all[1 - first, pl.ds(row, 32), :] = ref[k, 32:64, :]
    for slot, out in ((1, send), (0, keep)):
        w = w_all[slot]
        out[0:192] = dot(own_ref[...], w, NT).astype(BF16)
        out[192:384] = dot(mate_ref[...], w, NT).astype(BF16)


def positions(x, shape, dim):
    at = lax.broadcasted_iota(jnp.int32, shape, dim)
    first = x[192:200, 0:128].astype(F32).astype(jnp.int32)[0:1, 0:1]
    second = x[192:200, 384:512].astype(F32).astype(jnp.int32)[0:1, 0:1]
    return jnp.where(at < 96, first * 96 + at, second * 96 + (at - 96))


def forward_kernel(where, x_all, near, far, lse_ref, k_all, v_all):
    xs = [x_all.at[where[0] ^ i] for i in range(4)]
    for i, x in enumerate(xs):
        k_all[192 * i : 192 * i + 192] = x[0:192, 256:512]
        v_all[192 * i : 192 * i + 192] = x[0:192, 512:768]
    key_pos = jnp.concatenate([positions(x, (1, 192), 1) for x in xs], axis=1)
    for i, x in enumerate(xs):
        rows = slice(192 * i, 192 * i + 192)
        here = slice(192 * (i % 2), 192 * (i % 2) + 192)
        allowed = key_pos <= positions(x, (192, 1), 0)
        for h in range(2):
            cols = slice(HD * h, HD * h + HD)
            s = dot(x[0:192, cols], k_all[:, cols], NT) * SCALE
            s = jnp.where(allowed, s, -jnp.inf)
            top = jnp.max(s, axis=1, keepdims=True)
            e = jnp.exp(s - top)
            total = jnp.sum(e, axis=1, keepdims=True)
            p = (e * (1.0 / total)).astype(BF16)
            out = near if i < 2 else far
            out[here, cols] = dot(p, v_all[:, cols], NN).astype(BF16)
            lse_ref[rows, cols] = jnp.broadcast_to(top + jnp.log(total), (192, HD))


def backward_kernel(
    where, x_all, g_near, g_far, o_near, o_far, lse_ref, home, k_all, v_all, dk, dv
):
    xs = [x_all.at[where[0] ^ i] for i in range(4)]
    outs = [home.at[where[0] ^ i] for i in range(4)]
    for i, x in enumerate(xs):
        k_all[192 * i : 192 * i + 192] = x[0:192, 256:512]
        v_all[192 * i : 192 * i + 192] = x[0:192, 512:768]
    key_pos = jnp.concatenate([positions(x, (1, 192), 1) for x in xs], axis=1)
    for i, x in enumerate(xs):
        rows = slice(192 * i, 192 * i + 192)
        here = slice(192 * (i % 2), 192 * (i % 2) + 192)
        grads, attended = (g_near, o_near) if i < 2 else (g_far, o_far)
        allowed = key_pos <= positions(x, (192, 1), 0)
        for h in range(2):
            cols = slice(HD * h, HD * h + HD)
            q = x[0:192, cols]
            g = grads[here, cols]
            s = dot(q, k_all[:, cols], NT) * SCALE
            p = jnp.exp(jnp.where(allowed, s, -jnp.inf) - lse_ref[rows, HD * h : HD * h + 1])
            delta = jnp.sum(g.astype(F32) * attended[here, cols].astype(F32), axis=1, keepdims=True)
            dp = dot(g, v_all[:, cols], NT)
            ds = (p * (dp - delta)).astype(BF16)
            outs[i][:, cols] = (dot(ds, k_all[:, cols], NN) * SCALE).astype(BF16)
            pk = dot(ds, q, TN)
            pv = dot(p.astype(BF16), g, TN)
            if i == 0:
                dk[:, cols] = pk
                dv[:, cols] = pv
            else:
                dk[:, cols] += pk
                dv[:, cols] += pv
    for i, out in enumerate(outs):
        rows = slice(192 * i, 192 * i + 192)
        out[:, 256:512] = (dk[rows] * SCALE).astype(BF16)
        out[:, 512:768] = dv[rows].astype(BF16)


def weight_kernel(where, o_here, o_there, own_ref, mate_ref, keep, send):
    core = where[0]
    for slot, o in ((0, o_here), (1, o_there)):
        for x in range(4):
            cols = slice(512 * x, 512 * x + 512)
            t = dot(o[0:192], own_ref[:, cols], TN) + dot(o[192:384], mate_ref[:, cols], TN)
            t = t.astype(BF16)
            for y in range(4):
                t0 = t[64 * y : 64 * y + 32]
                t1 = t[64 * y + 32 : 64 * y + 64]
                keep[y, x, slot] = jnp.where(core == 0, t0, t1)
                send[y, x, slot] = jnp.where(core == 0, t1, t0)


def sum_kernel(parts, own, other):
    for slot, out in ((0, own), (1, other)):
        t = [parts[j, slot].astype(F32) for j in range(16)]
        while len(t) > 1:
            t = [t[i] + t[i + 1] for i in range(0, len(t), 2)]
        out[...] = t[0].astype(BF16)


def nearest(dests, source_of, n=16):
    pairs = []
    for row in range(4):
        takers = [d for d in dests if source_of(*d) == row]
        best = None
        for columns in itertools.permutations(range(4), len(takers)):
            steps = 0
            for (a, b), c in zip(takers, columns):
                gap = abs((4 * a + b) - (4 * row + c))
                steps += min(gap, n - gap) ** 2
            if best is None or steps < best[0]:
                best = (steps, columns)
        for (a, b), c in zip(takers, best[1]):
            pairs.append((c * 4 + row, b * 4 + a))
    return pairs


def swap(value, axis, mask, n):
    return lax.ppermute(value, axis, [(i, i ^ mask) for i in range(n)])


def scalars(*values):
    return jnp.stack(values).astype(jnp.int32)


def exchange(value, axes):
    return lax.all_to_all(value, axes, 0, 0, tiled=True)


def shards(query, key, value, out_weight, out_grad, block_ids):
    b, a = lax.axis_index("seq"), lax.axis_index("zh")
    y, core = lax.axis_index("y"), lax.axis_index("c")
    half, pair = b & 1, b >> 1
    places = [(i, j) for i in range(4) for j in range(4)]
    z = ("seq", "zh")

    grads = out_grad[0]

    first = lax.ppermute(
        out_weight, z, nearest([d for d in places if d[0] // 2 != d[1] % 2], lambda i, j: i ^ 2)
    )
    second = lax.ppermute(
        out_weight, z, nearest(places, lambda i, j: i ^ 1 if i // 2 == j % 2 else i ^ 3)
    )
    packed = pl.pallas_call(
        pack_kernel,
        out_shape=arr((4, 200, 768)),
        in_specs=[SMEM] + [pl.BlockSpec(memory_space=pl.ANY)] * 3,
        out_specs=VMEM,
        scratch_shapes=[pltpu.SemaphoreType.DMA((12,))],
        compiler_params=pltpu.CompilerParams(vmem_limit_bytes=60 * 1024 * 1024),
        cost_estimate=pl.CostEstimate(flops=1000, bytes_accessed=1000, transcendentals=0),
        name="pack",
    )(block_ids, query[0], key[0], value[0])
    rows = exchange(packed, "seq")
    grads, first, second = lax.optimization_barrier((grads, first, second))
    mate_grads = swap(grads, "seq", 1, 4)
    first = jnp.where((a >> 1) == half, out_weight, first)
    piece = jnp.concatenate([first, second], axis=0)
    pieces = [piece] + [swap(piece, "y", k, 4) for k in (1, 2, 3)]
    w_here = jnp.stack(pieces)
    w_there = swap(w_here, "c", 1, 2)

    g_near, g_send = call(
        project_kernel, [arr((384, 256))] * 2, 1, 4, "project", [pltpu.VMEM((2, 256, 2048), BF16)]
    )(scalars((a & 1) ^ pair, core, *(y ^ k for k in range(4))), grads, mate_grads, w_here, w_there)
    g_far = swap(g_send, "seq", 2, 4)
    kv = [pltpu.VMEM((768, 256), BF16)] * 2
    o_near, o_far, lse = call(
        forward_kernel, [arr((384, 256))] * 2 + [arr((768, 256), F32)], 1, 1, "forward", kv
    )(scalars(b), rows)
    o_there = swap(o_far, "seq", 2, 4)
    o_there, w_here = lax.optimization_barrier((o_there, w_here))
    keep, send = call(weight_kernel, [arr((4, 4, 2, 32, 512))] * 2, 1, 4, "weight")(
        scalars(core), o_near, o_there, grads, mate_grads
    )
    taken = swap(send, "c", 1, 2)
    back = call(
        backward_kernel,
        arr((4, 192, 768)),
        1,
        6,
        "backward",
        kv + [pltpu.VMEM((768, 256), F32)] * 2,
    )(scalars(b), rows, g_near, g_far, o_near, o_far, lse)
    home = exchange(back, "seq")
    both = (keep.astype(F32) + taken.astype(F32)).astype(BF16).reshape(16, 2, 32, 512)
    parts = exchange(both, ("y", "dp"))
    own, other = call(sum_kernel, [arr((32, 512))] * 2, 0, 1, "sum")(parts)
    turn = [(i * 4 + j, group_of(j) * 4 + group_of(i)) for i in range(4) for j in range(4)]
    turn2 = [(i * 4 + j, group_of(j) * 4 + (group_of(i) ^ 1)) for i in range(4) for j in range(4)]
    line = lax.ppermute(own, z, turn).astype(F32) + lax.ppermute(other, z, turn2).astype(F32)
    line, home = lax.optimization_barrier((line, home))
    spread = jnp.broadcast_to(line.astype(BF16)[None], (4, 32, 512))
    quarter = call(quarter_kernel, arr((4, 32, 512)), 0, 1, "quarter")(exchange(spread, "seq"))
    weight_grad = call(finish_kernel, arr((32, 2048)), 0, 1, "finish")(exchange(quarter, "dp"))
    query_grad, key_grad, value_grad = call(unpack_kernel, [arr((192, 1024))] * 3, 0, 1, "unpack")(
        home
    )
    return query_grad[None], key_grad[None], value_grad[None], weight_grad


def solution(mesh):
    fine = Mesh(mesh.devices.reshape(4, 4, 4, 2, 4), ("seq", "zh", "y", "c", "dp"))
    tokens = P(("zh", "y", "c", "dp"), "seq", None)
    rows = P(("zh", "y", "c"), None)
    return jax.shard_map(
        shards,
        mesh=fine,
        in_specs=(tokens, tokens, tokens, rows, tokens, P("seq")),
        out_specs=(tokens, tokens, tokens, rows),
        check_vma=False,
    )
```

```python
import itertools
import math

import jax
import jax.numpy as jnp
from jax import lax
from jax.experimental import pallas as pl
from jax.experimental.pallas import tpu as pltpu
from jax.sharding import Mesh
from jax.sharding import PartitionSpec as P

HD = 128
BF16 = jnp.bfloat16
F32 = jnp.float32
SCALE = 1.0 / math.sqrt(HD)
VMEM = pl.BlockSpec(memory_space=pltpu.VMEM)
SMEM = pl.BlockSpec(memory_space=pltpu.SMEM)
NT = (((1,), (1,)), ((), ()))
NN = (((1,), (0,)), ((), ()))
TN = (((0,), (0,)), ((), ()))


def dot(a, b, dims):
    return lax.dot_general(a, b, dims, preferred_element_type=F32)


def call(kernel, outs, n_scalar, n_vector, name, scratch=()):
    return pl.pallas_call(
        kernel,
        out_shape=outs,
        in_specs=[SMEM] * n_scalar + [VMEM] * n_vector,
        out_specs=jax.tree.map(lambda _: VMEM, outs),
        scratch_shapes=list(scratch),
        compiler_params=pltpu.CompilerParams(vmem_limit_bytes=40 * 1024 * 1024),
        cost_estimate=pl.CostEstimate(flops=1000, bytes_accessed=1000, transcendentals=0),
        name=name,
    )


def arr(shape, dtype=BF16):
    return jax.ShapeDtypeStruct(shape, dtype)


def group_of(b):
    return 2 * (b % 2) + b // 2


def pack_kernel(ids, q_ref, k_ref, v_ref, out, sems):
    copies = []
    for j in range(4):
        cols = pl.ds(256 * group_of(j), 256)
        for n, ref in enumerate((q_ref, k_ref, v_ref)):
            to = out.at[j, pl.ds(0, 192), pl.ds(256 * n, 256)]
            copies.append(pltpu.make_async_copy(ref.at[:, cols], to, sems.at[3 * j + n]))
            copies[-1].start()
    lane = lax.broadcasted_iota(jnp.int32, (8, 768), 1)
    block = jnp.where(lane < 384, ids[0], ids[1]).astype(F32).astype(BF16)
    for j in range(4):
        out[j, 192:200, :] = block
    for copy in copies:
        copy.wait()


def unpack_kernel(home, dq, dk, dv):
    for j in range(4):
        cols = slice(256 * group_of(j), 256 * group_of(j) + 256)
        dq[:, cols] = home[j, :, 0:256]
        dk[:, cols] = home[j, :, 256:512]
        dv[:, cols] = home[j, :, 512:768]


def quarter_kernel(parts, out):
    t = [parts[j].astype(F32) for j in range(4)]
    total = ((t[0] + t[1]) + (t[2] + t[3])) * (1.0 / math.sqrt(192 * 512))
    for x in range(4):
        out[x] = total.astype(BF16)


def finish_kernel(parts, out):
    for x in range(4):
        out[:, 512 * x : 512 * x + 512] = parts[x]


def project_kernel(where, own_ref, mate_ref, w_here, w_there, keep, send, w_all):
    first, core = where[0], where[1]
    for k in range(4):
        for c, ref in ((0, w_here), (1, w_there)):
            row = pl.multiple_of((2 * where[2 + k] + lax.rem(core + c, 2)) * 32, 32)
            w_all[first, pl.ds(row, 32), :] = ref[k, 0:32, :]
            w_all[1 - first, pl.ds(row, 32), :] = ref[k, 32:64, :]
    for slot, out in ((1, send), (0, keep)):
        w = w_all[slot]
        out[0:192] = dot(own_ref[...], w, NT).astype(BF16)
        out[192:384] = dot(mate_ref[...], w, NT).astype(BF16)


def positions(x, shape, dim):
    at = lax.broadcasted_iota(jnp.int32, shape, dim)
    first = x[192:200, 0:128].astype(F32).astype(jnp.int32)[0:1, 0:1]
    second = x[192:200, 384:512].astype(F32).astype(jnp.int32)[0:1, 0:1]
    return jnp.where(at < 96, first * 96 + at, second * 96 + (at - 96))


def forward_kernel(where, x_all, near, far, lse_ref, k_all, v_all):
    xs = [x_all.at[where[0] ^ i] for i in range(4)]
    for i, x in enumerate(xs):
        k_all[192 * i : 192 * i + 192] = x[0:192, 256:512]
        v_all[192 * i : 192 * i + 192] = x[0:192, 512:768]
    key_pos = jnp.concatenate([positions(x, (1, 192), 1) for x in xs], axis=1)
    for i, x in enumerate(xs):
        rows = slice(192 * i, 192 * i + 192)
        here = slice(192 * (i % 2), 192 * (i % 2) + 192)
        allowed = key_pos <= positions(x, (192, 1), 0)
        for h in range(2):
            cols = slice(HD * h, HD * h + HD)
            s = dot(x[0:192, cols], k_all[:, cols], NT) * SCALE
            s = jnp.where(allowed, s, -jnp.inf)
            top = jnp.max(s, axis=1, keepdims=True)
            e = jnp.exp(s - top)
            total = jnp.sum(e, axis=1, keepdims=True)
            p = (e * (1.0 / total)).astype(BF16)
            out = near if i < 2 else far
            out[here, cols] = dot(p, v_all[:, cols], NN).astype(BF16)
            lse_ref[rows, cols] = jnp.broadcast_to(top + jnp.log(total), (192, HD))


def backward_kernel(
    where, x_all, g_near, g_far, o_near, o_far, lse_ref, home, k_all, v_all, dk, dv
):
    xs = [x_all.at[where[0] ^ i] for i in range(4)]
    outs = [home.at[where[0] ^ i] for i in range(4)]
    for i, x in enumerate(xs):
        k_all[192 * i : 192 * i + 192] = x[0:192, 256:512]
        v_all[192 * i : 192 * i + 192] = x[0:192, 512:768]
    key_pos = jnp.concatenate([positions(x, (1, 192), 1) for x in xs], axis=1)
    for i, x in enumerate(xs):
        rows = slice(192 * i, 192 * i + 192)
        here = slice(192 * (i % 2), 192 * (i % 2) + 192)
        grads, attended = (g_near, o_near) if i < 2 else (g_far, o_far)
        allowed = key_pos <= positions(x, (192, 1), 0)
        for h in range(2):
            cols = slice(HD * h, HD * h + HD)
            q = x[0:192, cols]
            g = grads[here, cols]
            s = dot(q, k_all[:, cols], NT) * SCALE
            p = jnp.exp(jnp.where(allowed, s, -jnp.inf) - lse_ref[rows, HD * h : HD * h + 1])
            delta = jnp.sum(g.astype(F32) * attended[here, cols].astype(F32), axis=1, keepdims=True)
            dp = dot(g, v_all[:, cols], NT)
            ds = (p * (dp - delta)).astype(BF16)
            outs[i][:, cols] = (dot(ds, k_all[:, cols], NN) * SCALE).astype(BF16)
            pk = dot(ds, q, TN)
            pv = dot(p.astype(BF16), g, TN)
            if i == 0:
                dk[:, cols] = pk
                dv[:, cols] = pv
            else:
                dk[:, cols] += pk
                dv[:, cols] += pv
    for i, out in enumerate(outs):
        rows = slice(192 * i, 192 * i + 192)
        out[:, 256:512] = (dk[rows] * SCALE).astype(BF16)
        out[:, 512:768] = dv[rows].astype(BF16)


def weight_kernel(where, o_here, o_there, own_ref, mate_ref, keep, send):
    core = where[0]
    for slot, o in ((0, o_here), (1, o_there)):
        for x in range(4):
            cols = slice(512 * x, 512 * x + 512)
            t = dot(o[0:192], own_ref[:, cols], TN) + dot(o[192:384], mate_ref[:, cols], TN)
            t = t.astype(BF16)
            for y in range(4):
                t0 = t[64 * y : 64 * y + 32]
                t1 = t[64 * y + 32 : 64 * y + 64]
                keep[y, x, slot] = jnp.where(core == 0, t0, t1)
                send[y, x, slot] = jnp.where(core == 0, t1, t0)


def sum_kernel(parts, own, other):
    for slot, out in ((0, own), (1, other)):
        t = [parts[j, slot].astype(F32) for j in range(16)]
        while len(t) > 1:
            t = [t[i] + t[i + 1] for i in range(0, len(t), 2)]
        out[...] = t[0].astype(BF16)


def nearest(dests, source_of, n=16):
    pairs = []
    for row in range(4):
        takers = [d for d in dests if source_of(*d) == row]
        best = None
        for columns in itertools.permutations(range(4), len(takers)):
            steps = 0
            for (a, b), c in zip(takers, columns):
                gap = abs((4 * a + b) - (4 * row + c))
                steps += min(gap, n - gap) ** 2
            if best is None or steps < best[0]:
                best = (steps, columns)
        for (a, b), c in zip(takers, best[1]):
            pairs.append((c * 4 + row, b * 4 + a))
    return pairs


def swap(value, axis, mask, n):
    return lax.ppermute(value, axis, [(i, i ^ mask) for i in range(n)])


def scalars(*values):
    return jnp.stack(values).astype(jnp.int32)


def exchange(value, axes):
    return lax.all_to_all(value, axes, 0, 0, tiled=True)


def shards(query, key, value, out_weight, out_grad, block_ids):
    b, a = lax.axis_index("seq"), lax.axis_index("zh")
    y, core = lax.axis_index("y"), lax.axis_index("c")
    half, pair = b & 1, b >> 1
    places = [(i, j) for i in range(4) for j in range(4)]
    z = ("seq", "zh")

    grads = out_grad[0]

    first = lax.ppermute(
        out_weight, z, nearest([d for d in places if d[0] // 2 != d[1] % 2], lambda i, j: i ^ 2)
    )
    second = lax.ppermute(
        out_weight, z, nearest(places, lambda i, j: i ^ 1 if i // 2 == j % 2 else i ^ 3)
    )
    packed = pl.pallas_call(
        pack_kernel,
        out_shape=arr((4, 200, 768)),
        in_specs=[SMEM] + [pl.BlockSpec(memory_space=pl.ANY)] * 3,
        out_specs=VMEM,
        scratch_shapes=[pltpu.SemaphoreType.DMA((12,))],
        compiler_params=pltpu.CompilerParams(vmem_limit_bytes=60 * 1024 * 1024),
        cost_estimate=pl.CostEstimate(flops=1000, bytes_accessed=1000, transcendentals=0),
        name="pack",
    )(block_ids, query[0], key[0], value[0])
    rows = exchange(packed, "seq")
    mate_grads = swap(grads, "seq", 1, 4)
    first = jnp.where((a >> 1) == half, out_weight, first)
    piece = jnp.concatenate([first, second], axis=0)
    pieces = [piece] + [swap(piece, "y", k, 4) for k in (1, 2, 3)]
    w_here = jnp.stack(pieces)
    w_there = swap(w_here, "c", 1, 2)

    g_near, g_send = call(
        project_kernel, [arr((384, 256))] * 2, 1, 4, "project", [pltpu.VMEM((2, 256, 2048), BF16)]
    )(scalars((a & 1) ^ pair, core, *(y ^ k for k in range(4))), grads, mate_grads, w_here, w_there)
    g_far = swap(g_send, "seq", 2, 4)
    kv = [pltpu.VMEM((768, 256), BF16)] * 2
    o_near, o_far, lse = call(
        forward_kernel, [arr((384, 256))] * 2 + [arr((768, 256), F32)], 1, 1, "forward", kv
    )(scalars(b), rows)
    o_there = swap(o_far, "seq", 2, 4)
    o_there, w_here = lax.optimization_barrier((o_there, w_here))
    keep, send = call(weight_kernel, [arr((4, 4, 2, 32, 512))] * 2, 1, 4, "weight")(
        scalars(core), o_near, o_there, grads, mate_grads
    )
    taken = swap(send, "c", 1, 2)
    back = call(
        backward_kernel,
        arr((4, 192, 768)),
        1,
        6,
        "backward",
        kv + [pltpu.VMEM((768, 256), F32)] * 2,
    )(scalars(b), rows, g_near, g_far, o_near, o_far, lse)
    home = exchange(back, "seq")
    both = (keep.astype(F32) + taken.astype(F32)).astype(BF16).reshape(16, 2, 32, 512)
    parts = exchange(both, ("y", "dp"))
    own, other = call(sum_kernel, [arr((32, 512))] * 2, 0, 1, "sum")(parts)
    turn = [(i * 4 + j, group_of(j) * 4 + group_of(i)) for i in range(4) for j in range(4)]
    turn2 = [(i * 4 + j, group_of(j) * 4 + (group_of(i) ^ 1)) for i in range(4) for j in range(4)]
    line = lax.ppermute(own, z, turn).astype(F32) + lax.ppermute(other, z, turn2).astype(F32)
    line, home = lax.optimization_barrier((line, home))
    spread = jnp.broadcast_to(line.astype(BF16)[None], (4, 32, 512))
    quarter = call(quarter_kernel, arr((4, 32, 512)), 0, 1, "quarter")(exchange(spread, "seq"))
    weight_grad = call(finish_kernel, arr((32, 2048)), 0, 1, "finish")(exchange(quarter, "dp"))
    query_grad, key_grad, value_grad = call(unpack_kernel, [arr((192, 1024))] * 3, 0, 1, "unpack")(
        home
    )
    return query_grad[None], key_grad[None], value_grad[None], weight_grad


def solution(mesh):
    fine = Mesh(mesh.devices.reshape(4, 4, 4, 2, 4), ("seq", "zh", "y", "c", "dp"))
    tokens = P(("zh", "y", "c", "dp"), "seq", None)
    rows = P(("zh", "y", "c"), None)
    return jax.shard_map(
        shards,
        mesh=fine,
        in_specs=(tokens, tokens, tokens, rows, tokens, P("seq")),
        out_specs=(tokens, tokens, tokens, rows),
        check_vma=False,
    )
```

```python
import functools
import itertools
import math

import jax
import jax.numpy as jnp
from jax import lax
from jax.experimental import pallas as pl
from jax.experimental.pallas import tpu as pltpu
from jax.sharding import Mesh
from jax.sharding import PartitionSpec as P

HD = 128
BF16 = jnp.bfloat16
F32 = jnp.float32
SCALE = 1.0 / math.sqrt(HD)
VMEM = pl.BlockSpec(memory_space=pltpu.VMEM)
SMEM = pl.BlockSpec(memory_space=pltpu.SMEM)
NT = (((1,), (1,)), ((), ()))
NN = (((1,), (0,)), ((), ()))
TN = (((0,), (0,)), ((), ()))


def dot(a, b, dims):
    return lax.dot_general(a, b, dims, preferred_element_type=F32)


def call(kernel, outs, n_scalar, n_vector, name, scratch=()):
    return pl.pallas_call(
        kernel,
        out_shape=outs,
        in_specs=[SMEM] * n_scalar + [VMEM] * n_vector,
        out_specs=jax.tree.map(lambda _: VMEM, outs),
        scratch_shapes=list(scratch),
        compiler_params=pltpu.CompilerParams(vmem_limit_bytes=40 * 1024 * 1024),
        cost_estimate=pl.CostEstimate(flops=1000, bytes_accessed=1000, transcendentals=0),
        name=name,
    )


def arr(shape, dtype=BF16):
    return jax.ShapeDtypeStruct(shape, dtype)


def group_of(b):
    return 2 * (b % 2) + b // 2


def pack_kernel(ids, q_ref, k_ref, v_ref, out, sems):
    copies = []
    for j in range(4):
        cols = pl.ds(256 * group_of(j), 256)
        for n, ref in enumerate((q_ref, k_ref, v_ref)):
            to = out.at[j, pl.ds(0, 192), pl.ds(256 * n, 256)]
            copies.append(pltpu.make_async_copy(ref.at[:, cols], to, sems.at[3 * j + n]))
            copies[-1].start()
    lane = lax.broadcasted_iota(jnp.int32, (8, 768), 1)
    block = jnp.where(lane < 384, ids[0], ids[1]).astype(F32).astype(BF16)
    for j in range(4):
        out[j, 192:200, :] = block
    for copy in copies:
        copy.wait()


def unpack_kernel(home, dq, dk, dv):
    for j in range(4):
        cols = slice(256 * group_of(j), 256 * group_of(j) + 256)
        dq[:, cols] = home[j, :, 0:256]
        dk[:, cols] = home[j, :, 256:512]
        dv[:, cols] = home[j, :, 512:768]


def quarter_kernel(parts, out):
    t = [parts[j].astype(F32) for j in range(4)]
    total = ((t[0] + t[1]) + (t[2] + t[3])) * (1.0 / math.sqrt(192 * 512))
    for x in range(4):
        out[x] = total.astype(BF16)


def finish_kernel(parts, out):
    for x in range(4):
        out[:, 512 * x : 512 * x + 512] = parts[x]


def project_kernel(where, own_ref, mate_ref, w_here, w_there, keep, send, w_all):
    first, core = where[0], where[1]
    for k in range(4):
        for c, ref in ((0, w_here), (1, w_there)):
            row = pl.multiple_of((2 * where[2 + k] + lax.rem(core + c, 2)) * 32, 32)
            w_all[first, pl.ds(row, 32), :] = ref[k, 0:32, :]
            w_all[1 - first, pl.ds(row, 32), :] = ref[k, 32:64, :]
    for slot, out in ((1, send), (0, keep)):
        w = w_all[slot]
        out[0:192] = dot(own_ref[...], w, NT).astype(BF16)
        out[192:384] = dot(mate_ref[...], w, NT).astype(BF16)


def positions(x, shape, dim):
    at = lax.broadcasted_iota(jnp.int32, shape, dim)
    first = x[192:200, 0:128].astype(F32).astype(jnp.int32)[0:1, 0:1]
    second = x[192:200, 384:512].astype(F32).astype(jnp.int32)[0:1, 0:1]
    return jnp.where(at < 96, first * 96 + at, second * 96 + (at - 96))


def forward_kernel(first, where, x_all, out, lse_ref, k_all, v_all):
    xs = [x_all.at[where[0] ^ i] for i in range(4)]
    for i, x in enumerate(xs):
        k_all[192 * i : 192 * i + 192] = x[0:192, 256:512]
        v_all[192 * i : 192 * i + 192] = x[0:192, 512:768]
    key_pos = jnp.concatenate([positions(x, (1, 192), 1) for x in xs], axis=1)
    for i in (first, first + 1):
        x = xs[i]
        here = slice(192 * (i % 2), 192 * (i % 2) + 192)
        allowed = key_pos <= positions(x, (192, 1), 0)
        for h in range(2):
            cols = slice(HD * h, HD * h + HD)
            s = dot(x[0:192, cols], k_all[:, cols], NT) * SCALE
            s = jnp.where(allowed, s, -jnp.inf)
            top = jnp.max(s, axis=1, keepdims=True)
            e = jnp.exp(s - top)
            total = jnp.sum(e, axis=1, keepdims=True)
            p = (e * (1.0 / total)).astype(BF16)
            out[here, cols] = dot(p, v_all[:, cols], NN).astype(BF16)
            lse_ref[here, cols] = jnp.broadcast_to(top + jnp.log(total), (192, HD))


def backward_kernel(
    where, x_all, g_near, g_far, o_near, o_far, lse_near, lse_far, home, k_all, v_all, dk, dv
):
    xs = [x_all.at[where[0] ^ i] for i in range(4)]
    outs = [home.at[where[0] ^ i] for i in range(4)]
    for i, x in enumerate(xs):
        k_all[192 * i : 192 * i + 192] = x[0:192, 256:512]
        v_all[192 * i : 192 * i + 192] = x[0:192, 512:768]
    key_pos = jnp.concatenate([positions(x, (1, 192), 1) for x in xs], axis=1)
    for i, x in enumerate(xs):
        lse_ref = lse_near if i < 2 else lse_far
        here = slice(192 * (i % 2), 192 * (i % 2) + 192)
        grads, attended = (g_near, o_near) if i < 2 else (g_far, o_far)
        allowed = key_pos <= positions(x, (192, 1), 0)
        for h in range(2):
            cols = slice(HD * h, HD * h + HD)
            q = x[0:192, cols]
            g = grads[here, cols]
            s = dot(q, k_all[:, cols], NT) * SCALE
            p = jnp.exp(jnp.where(allowed, s, -jnp.inf) - lse_ref[here, HD * h : HD * h + 1])
            delta = jnp.sum(g.astype(F32) * attended[here, cols].astype(F32), axis=1, keepdims=True)
            dp = dot(g, v_all[:, cols], NT)
            ds = (p * (dp - delta)).astype(BF16)
            outs[i][:, cols] = (dot(ds, k_all[:, cols], NN) * SCALE).astype(BF16)
            pk = dot(ds, q, TN)
            pv = dot(p.astype(BF16), g, TN)
            if i == 0:
                dk[:, cols] = pk
                dv[:, cols] = pv
            else:
                dk[:, cols] += pk
                dv[:, cols] += pv
    for i, out in enumerate(outs):
        rows = slice(192 * i, 192 * i + 192)
        out[:, 256:512] = (dk[rows] * SCALE).astype(BF16)
        out[:, 512:768] = dv[rows].astype(BF16)


def weight_kernel(where, o_here, o_there, own_ref, mate_ref, keep, send):
    core = where[0]
    for slot, o in ((0, o_here), (1, o_there)):
        for x in range(4):
            cols = slice(512 * x, 512 * x + 512)
            t = dot(o[0:192], own_ref[:, cols], TN) + dot(o[192:384], mate_ref[:, cols], TN)
            t = t.astype(BF16)
            for y in range(4):
                t0 = t[64 * y : 64 * y + 32]
                t1 = t[64 * y + 32 : 64 * y + 64]
                keep[y, x, slot] = jnp.where(core == 0, t0, t1)
                send[y, x, slot] = jnp.where(core == 0, t1, t0)


def sum_kernel(parts, own, other):
    for slot, out in ((0, own), (1, other)):
        t = [parts[j, slot].astype(F32) for j in range(16)]
        while len(t) > 1:
            t = [t[i] + t[i + 1] for i in range(0, len(t), 2)]
        out[...] = t[0].astype(BF16)


def nearest(dests, source_of, n=16):
    pairs = []
    for row in range(4):
        takers = [d for d in dests if source_of(*d) == row]
        best = None
        for columns in itertools.permutations(range(4), len(takers)):
            steps = 0
            for (a, b), c in zip(takers, columns):
                gap = abs((4 * a + b) - (4 * row + c))
                steps += min(gap, n - gap) ** 2
            if best is None or steps < best[0]:
                best = (steps, columns)
        for (a, b), c in zip(takers, best[1]):
            pairs.append((c * 4 + row, b * 4 + a))
    return pairs


def swap(value, axis, mask, n):
    return lax.ppermute(value, axis, [(i, i ^ mask) for i in range(n)])


def scalars(*values):
    return jnp.stack(values).astype(jnp.int32)


def exchange(value, axes):
    return lax.all_to_all(value, axes, 0, 0, tiled=True)


def shards(query, key, value, out_weight, out_grad, block_ids):
    b, a = lax.axis_index("seq"), lax.axis_index("zh")
    y, core = lax.axis_index("y"), lax.axis_index("c")
    half, pair = b & 1, b >> 1
    places = [(i, j) for i in range(4) for j in range(4)]
    z = ("seq", "zh")

    grads = out_grad[0]

    first = lax.ppermute(
        out_weight, z, nearest([d for d in places if d[0] // 2 != d[1] % 2], lambda i, j: i ^ 2)
    )
    second = lax.ppermute(
        out_weight, z, nearest(places, lambda i, j: i ^ 1 if i // 2 == j % 2 else i ^ 3)
    )
    packed = pl.pallas_call(
        pack_kernel,
        out_shape=arr((4, 200, 768)),
        in_specs=[SMEM] + [pl.BlockSpec(memory_space=pl.ANY)] * 3,
        out_specs=VMEM,
        scratch_shapes=[pltpu.SemaphoreType.DMA((12,))],
        compiler_params=pltpu.CompilerParams(vmem_limit_bytes=60 * 1024 * 1024),
        cost_estimate=pl.CostEstimate(flops=1000, bytes_accessed=1000, transcendentals=0),
        name="pack",
    )(block_ids, query[0], key[0], value[0])
    rows = exchange(packed, "seq")
    mate_grads = swap(grads, "seq", 1, 4)
    first = jnp.where((a >> 1) == half, out_weight, first)
    piece = jnp.concatenate([first, second], axis=0)
    pieces = [piece] + [swap(piece, "y", k, 4) for k in (1, 2, 3)]
    w_here = jnp.stack(pieces)
    w_there = swap(w_here, "c", 1, 2)

    g_near, g_send = call(
        project_kernel, [arr((384, 256))] * 2, 1, 4, "project", [pltpu.VMEM((2, 256, 2048), BF16)]
    )(scalars((a & 1) ^ pair, core, *(y ^ k for k in range(4))), grads, mate_grads, w_here, w_there)
    g_far = swap(g_send, "seq", 2, 4)
    kv = [pltpu.VMEM((768, 256), BF16)] * 2
    halves = [arr((384, 256)), arr((384, 256), F32)]
    o_far, lse_far = call(functools.partial(forward_kernel, 2), halves, 1, 1, "far", kv)(
        scalars(b), rows
    )
    o_near, lse_near = call(functools.partial(forward_kernel, 0), halves, 1, 1, "near", kv)(
        scalars(b), rows
    )
    o_there = swap(o_far, "seq", 2, 4)
    o_there, w_here = lax.optimization_barrier((o_there, w_here))
    keep, send = call(weight_kernel, [arr((4, 4, 2, 32, 512))] * 2, 1, 4, "weight")(
        scalars(core), o_near, o_there, grads, mate_grads
    )
    taken = swap(send, "c", 1, 2)
    back = call(
        backward_kernel,
        arr((4, 192, 768)),
        1,
        7,
        "backward",
        kv + [pltpu.VMEM((768, 256), F32)] * 2,
    )(scalars(b), rows, g_near, g_far, o_near, o_far, lse_near, lse_far)
    home = exchange(back, "seq")
    both = (keep.astype(F32) + taken.astype(F32)).astype(BF16).reshape(16, 2, 32, 512)
    parts = exchange(both, ("y", "dp"))
    own, other = call(sum_kernel, [arr((32, 512))] * 2, 0, 1, "sum")(parts)
    turn = [(i * 4 + j, group_of(j) * 4 + group_of(i)) for i in range(4) for j in range(4)]
    turn2 = [(i * 4 + j, group_of(j) * 4 + (group_of(i) ^ 1)) for i in range(4) for j in range(4)]
    line = lax.ppermute(own, z, turn).astype(F32) + lax.ppermute(other, z, turn2).astype(F32)
    line, home = lax.optimization_barrier((line, home))
    spread = jnp.broadcast_to(line.astype(BF16)[None], (4, 32, 512))
    quarter = call(quarter_kernel, arr((4, 32, 512)), 0, 1, "quarter")(exchange(spread, "seq"))
    weight_grad = call(finish_kernel, arr((32, 2048)), 0, 1, "finish")(exchange(quarter, "dp"))
    query_grad, key_grad, value_grad = call(unpack_kernel, [arr((192, 1024))] * 3, 0, 1, "unpack")(
        home
    )
    return query_grad[None], key_grad[None], value_grad[None], weight_grad


def solution(mesh):
    fine = Mesh(mesh.devices.reshape(4, 4, 4, 2, 4), ("seq", "zh", "y", "c", "dp"))
    tokens = P(("zh", "y", "c", "dp"), "seq", None)
    rows = P(("zh", "y", "c"), None)
    return jax.shard_map(
        shards,
        mesh=fine,
        in_specs=(tokens, tokens, tokens, rows, tokens, P("seq")),
        out_specs=(tokens, tokens, tokens, rows),
        check_vma=False,
    )
```

```python
import functools
import itertools
import math

import jax
import jax.numpy as jnp
from jax import lax
from jax.experimental import pallas as pl
from jax.experimental.pallas import tpu as pltpu
from jax.sharding import Mesh
from jax.sharding import PartitionSpec as P

HD = 128
BF16 = jnp.bfloat16
F32 = jnp.float32
SCALE = 1.0 / math.sqrt(HD)
VMEM = pl.BlockSpec(memory_space=pltpu.VMEM)
SMEM = pl.BlockSpec(memory_space=pltpu.SMEM)
NT = (((1,), (1,)), ((), ()))
NN = (((1,), (0,)), ((), ()))
TN = (((0,), (0,)), ((), ()))


def dot(a, b, dims):
    return lax.dot_general(a, b, dims, preferred_element_type=F32)


def call(kernel, outs, n_scalar, n_vector, name, scratch=()):
    return pl.pallas_call(
        kernel,
        out_shape=outs,
        in_specs=[SMEM] * n_scalar + [VMEM] * n_vector,
        out_specs=jax.tree.map(lambda _: VMEM, outs),
        scratch_shapes=list(scratch),
        compiler_params=pltpu.CompilerParams(vmem_limit_bytes=56 * 1024 * 1024),
        cost_estimate=pl.CostEstimate(flops=1000, bytes_accessed=1000, transcendentals=0),
        name=name,
    )


def arr(shape, dtype=BF16):
    return jax.ShapeDtypeStruct(shape, dtype)


def group_of(b):
    return 2 * (b % 2) + b // 2


def pack_kernel(ids, q_ref, k_ref, v_ref, out, sems):
    copies = []
    for j in range(4):
        cols = pl.ds(256 * group_of(j), 256)
        for n, ref in enumerate((q_ref, k_ref, v_ref)):
            to = out.at[j, pl.ds(0, 192), pl.ds(256 * n, 256)]
            copies.append(pltpu.make_async_copy(ref.at[:, cols], to, sems.at[3 * j + n]))
            copies[-1].start()
    lane = lax.broadcasted_iota(jnp.int32, (8, 768), 1)
    block = jnp.where(lane < 384, ids[0], ids[1]).astype(F32).astype(BF16)
    for j in range(4):
        out[j, 192:200, :] = block
    for copy in copies:
        copy.wait()


def unpack_kernel(home, dq, dk, dv):
    for j in range(4):
        cols = slice(256 * group_of(j), 256 * group_of(j) + 256)
        dq[:, cols] = home[j, :, 0:256]
        dk[:, cols] = home[j, :, 256:512]
        dv[:, cols] = home[j, :, 512:768]


def quarter_kernel(parts, out):
    t = [parts[j].astype(F32) for j in range(4)]
    total = ((t[0] + t[1]) + (t[2] + t[3])) * (1.0 / math.sqrt(192 * 512))
    for x in range(4):
        out[x] = total.astype(BF16)


def finish_kernel(parts, out):
    for x in range(4):
        out[:, 512 * x : 512 * x + 512] = parts[x]


def project_kernel(where, own_ref, mate_ref, w_here, w_there, keep, send, w_all):
    first, core = where[0], where[1]
    for k in range(4):
        for c, ref in ((0, w_here), (1, w_there)):
            row = pl.multiple_of((2 * where[2 + k] + lax.rem(core + c, 2)) * 32, 32)
            w_all[first, pl.ds(row, 32), :] = ref[k, 0:32, :]
            w_all[1 - first, pl.ds(row, 32), :] = ref[k, 32:64, :]
    for slot, out in ((1, send), (0, keep)):
        w = w_all[slot]
        out[0:192] = dot(own_ref[...], w, NT).astype(BF16)
        out[192:384] = dot(mate_ref[...], w, NT).astype(BF16)


def positions(x, shape, dim):
    at = lax.broadcasted_iota(jnp.int32, shape, dim)
    first = x[192:200, 0:128].astype(F32).astype(jnp.int32)[0:1, 0:1]
    second = x[192:200, 384:512].astype(F32).astype(jnp.int32)[0:1, 0:1]
    return jnp.where(at < 96, first * 96 + at, second * 96 + (at - 96))


def forward_kernel(first, where, x_all, out, lse_ref, k_all, v_all):
    xs = [x_all.at[where[0] ^ i] for i in range(4)]
    for i, x in enumerate(xs):
        k_all[192 * i : 192 * i + 192] = x[0:192, 256:512]
        v_all[192 * i : 192 * i + 192] = x[0:192, 512:768]
    key_pos = jnp.concatenate([positions(x, (1, 192), 1) for x in xs], axis=1)
    for i in (first, first + 1):
        x = xs[i]
        here = slice(192 * (i % 2), 192 * (i % 2) + 192)
        allowed = key_pos <= positions(x, (192, 1), 0)
        for h in range(2):
            cols = slice(HD * h, HD * h + HD)
            s = dot(x[0:192, cols], k_all[:, cols], NT) * SCALE
            s = jnp.where(allowed, s, -jnp.inf)
            top = jnp.max(s, axis=1, keepdims=True)
            e = jnp.exp(s - top)
            total = jnp.sum(e, axis=1, keepdims=True)
            p = (e * (1.0 / total)).astype(BF16)
            out[here, cols] = dot(p, v_all[:, cols], NN).astype(BF16)
            lse_ref[here, cols] = jnp.broadcast_to(top + jnp.log(total), (192, HD))


def backward_kernel(
    where, x_all, g_near, g_far, o_near, o_far, lse_near, lse_far, home, k_all, v_all, dk, dv
):
    xs = [x_all.at[where[0] ^ i] for i in range(4)]
    outs = [home.at[where[0] ^ i] for i in range(4)]
    for i, x in enumerate(xs):
        k_all[192 * i : 192 * i + 192] = x[0:192, 256:512]
        v_all[192 * i : 192 * i + 192] = x[0:192, 512:768]
    key_pos = jnp.concatenate([positions(x, (1, 192), 1) for x in xs], axis=1)
    for i, x in enumerate(xs):
        lse_ref = lse_near if i < 2 else lse_far
        here = slice(192 * (i % 2), 192 * (i % 2) + 192)
        grads, attended = (g_near, o_near) if i < 2 else (g_far, o_far)
        allowed = key_pos <= positions(x, (192, 1), 0)
        for h in range(2):
            cols = slice(HD * h, HD * h + HD)
            q = x[0:192, cols]
            g = grads[here, cols]
            s = dot(q, k_all[:, cols], NT) * SCALE
            p = jnp.exp(jnp.where(allowed, s, -jnp.inf) - lse_ref[here, HD * h : HD * h + 1])
            delta = jnp.sum(g.astype(F32) * attended[here, cols].astype(F32), axis=1, keepdims=True)
            dp = dot(g, v_all[:, cols], NT)
            ds = (p * (dp - delta)).astype(BF16)
            outs[i][:, cols] = (dot(ds, k_all[:, cols], NN) * SCALE).astype(BF16)
            pk = dot(ds, q, TN)
            pv = dot(p.astype(BF16), g, TN)
            if i == 0:
                dk[:, cols] = pk
                dv[:, cols] = pv
            else:
                dk[:, cols] += pk
                dv[:, cols] += pv
    for i, out in enumerate(outs):
        rows = slice(192 * i, 192 * i + 192)
        out[:, 256:512] = (dk[rows] * SCALE).astype(BF16)
        out[:, 512:768] = dv[rows].astype(BF16)


def weight_kernel(where, o_here, o_there, own_ref, mate_ref, keep, send):
    core = where[0]
    for slot, o in ((0, o_here), (1, o_there)):
        for x in range(4):
            cols = slice(512 * x, 512 * x + 512)
            t = dot(o[0:192], own_ref[:, cols], TN) + dot(o[192:384], mate_ref[:, cols], TN)
            t = t.astype(BF16)
            for y in range(4):
                t0 = t[64 * y : 64 * y + 32]
                t1 = t[64 * y + 32 : 64 * y + 64]
                keep[y, x, slot] = jnp.where(core == 0, t0, t1)
                send[y, x, slot] = jnp.where(core == 0, t1, t0)


def sum_kernel(parts, own, other):
    for slot, out in ((0, own), (1, other)):
        t = [parts[j, slot].astype(F32) for j in range(16)]
        while len(t) > 1:
            t = [t[i] + t[i + 1] for i in range(0, len(t), 2)]
        out[...] = t[0].astype(BF16)


def nearest(dests, source_of, n=16):
    pairs = []
    for row in range(4):
        takers = [d for d in dests if source_of(*d) == row]
        best = None
        for columns in itertools.permutations(range(4), len(takers)):
            steps = 0
            for (a, b), c in zip(takers, columns):
                gap = abs((4 * a + b) - (4 * row + c))
                steps += min(gap, n - gap) ** 2
            if best is None or steps < best[0]:
                best = (steps, columns)
        for (a, b), c in zip(takers, best[1]):
            pairs.append((c * 4 + row, b * 4 + a))
    return pairs


def swap(value, axis, mask, n):
    return lax.ppermute(value, axis, [(i, i ^ mask) for i in range(n)])


def scalars(*values):
    return jnp.stack(values).astype(jnp.int32)


def exchange(value, axes):
    return lax.all_to_all(value, axes, 0, 0, tiled=True)


def shards(query, key, value, out_weight, out_grad, block_ids):
    b, a = lax.axis_index("seq"), lax.axis_index("zh")
    y, core = lax.axis_index("y"), lax.axis_index("c")
    half, pair = b & 1, b >> 1
    places = [(i, j) for i in range(4) for j in range(4)]
    z = ("seq", "zh")

    grads = out_grad[0]

    first = lax.ppermute(
        out_weight, z, nearest([d for d in places if d[0] // 2 != d[1] % 2], lambda i, j: i ^ 2)
    )
    second = lax.ppermute(
        out_weight, z, nearest(places, lambda i, j: i ^ 1 if i // 2 == j % 2 else i ^ 3)
    )
    packed = pl.pallas_call(
        pack_kernel,
        out_shape=arr((4, 200, 768)),
        in_specs=[SMEM] + [pl.BlockSpec(memory_space=pl.ANY)] * 3,
        out_specs=VMEM,
        scratch_shapes=[pltpu.SemaphoreType.DMA((12,))],
        compiler_params=pltpu.CompilerParams(vmem_limit_bytes=60 * 1024 * 1024),
        cost_estimate=pl.CostEstimate(flops=1000, bytes_accessed=1000, transcendentals=0),
        name="pack",
    )(block_ids, query[0], key[0], value[0])
    rows = exchange(packed, "seq")
    mate_grads = swap(grads, "seq", 1, 4)
    first = jnp.where((a >> 1) == half, out_weight, first)
    piece = jnp.concatenate([first, second], axis=0)
    pieces = [piece] + [swap(piece, "y", k, 4) for k in (1, 2, 3)]
    w_here = jnp.stack(pieces)
    w_there = swap(w_here, "c", 1, 2)

    g_near, g_send = call(
        project_kernel, [arr((384, 256))] * 2, 1, 4, "project", [pltpu.VMEM((2, 256, 2048), BF16)]
    )(scalars((a & 1) ^ pair, core, *(y ^ k for k in range(4))), grads, mate_grads, w_here, w_there)
    g_far = swap(g_send, "seq", 2, 4)
    kv = [pltpu.VMEM((768, 256), BF16)] * 2
    halves = [arr((384, 256)), arr((384, 256), F32)]
    o_far, lse_far = call(functools.partial(forward_kernel, 2), halves, 1, 1, "far", kv)(
        scalars(b), rows
    )
    o_near, lse_near = call(functools.partial(forward_kernel, 0), halves, 1, 1, "near", kv)(
        scalars(b), rows
    )
    o_there = swap(o_far, "seq", 2, 4)
    o_there, w_here = lax.optimization_barrier((o_there, w_here))
    keep, send = call(weight_kernel, [arr((4, 4, 2, 32, 512))] * 2, 1, 4, "weight")(
        scalars(core), o_near, o_there, grads, mate_grads
    )
    taken = swap(send, "c", 1, 2)
    back = call(
        backward_kernel,
        arr((4, 192, 768)),
        1,
        7,
        "backward",
        kv + [pltpu.VMEM((768, 256), F32)] * 2,
    )(scalars(b), rows, g_near, g_far, o_near, o_far, lse_near, lse_far)
    home = exchange(back, "seq")
    both = (keep.astype(F32) + taken.astype(F32)).astype(BF16).reshape(16, 2, 32, 512)
    parts = exchange(both, ("y", "dp"))
    own, other = call(sum_kernel, [arr((32, 512))] * 2, 0, 1, "sum")(parts)
    turn = [(i * 4 + j, group_of(j) * 4 + group_of(i)) for i in range(4) for j in range(4)]
    turn2 = [(i * 4 + j, group_of(j) * 4 + (group_of(i) ^ 1)) for i in range(4) for j in range(4)]
    line = lax.ppermute(own, z, turn).astype(F32) + lax.ppermute(other, z, turn2).astype(F32)
    line, home = lax.optimization_barrier((line, home))
    spread = jnp.broadcast_to(line.astype(BF16)[None], (4, 32, 512))
    quarter = call(quarter_kernel, arr((4, 32, 512)), 0, 1, "quarter")(exchange(spread, "seq"))
    weight_grad = call(finish_kernel, arr((32, 2048)), 0, 1, "finish")(exchange(quarter, "dp"))
    query_grad, key_grad, value_grad = call(unpack_kernel, [arr((192, 1024))] * 3, 0, 1, "unpack")(
        home
    )
    return query_grad[None], key_grad[None], value_grad[None], weight_grad


def solution(mesh):
    fine = Mesh(mesh.devices.reshape(4, 4, 4, 2, 4), ("seq", "zh", "y", "c", "dp"))
    tokens = P(("zh", "y", "c", "dp"), "seq", None)
    rows = P(("zh", "y", "c"), None)
    return jax.shard_map(
        shards,
        mesh=fine,
        in_specs=(tokens, tokens, tokens, rows, tokens, P("seq")),
        out_specs=(tokens, tokens, tokens, rows),
        check_vma=False,
    )
```
